512 devices in a mesh: dom: 16 (over z_hi, y), rel: 32 (over z_lo, x, core).
Axes of the slice: x: 4, y: 8, z: 8 (z_hi: 2, z_lo: 4; z = z_hi * 4 + z_lo), core: 2. Of those that a mesh axis runs over, the one named last changes fastest.
Arguments:
- entity: float32 [65536, 512], P(('dom', 'rel')), may hold values from -1.8 to 1.8
- entity_acc: float32 [65536, 512], P(('dom', 'rel')), may hold values from 0.01 to 1
- relation: float32 [4096, 512], P('rel'), may hold values from -1 to 1, as said below
- relation_acc: float32 [4096, 512], P('rel'), may hold values from 0.01 to 1
- send_rows: int32 [512, 32, 16], P(('dom', 'rel')), may hold values from 0 to 127, as said below
- trip_head: int32 [131072], P(('dom', 'rel')), may hold values from 0 to 511
- trip_rel: int32 [131072], P(('dom', 'rel')), may hold values from 0 to 127
- trip_tail: int32 [131072], P(('dom', 'rel')), may hold values from 0 to 511
- neg_part: int32 [1], replicated, may hold values from 0 to 15
- neg_rows: int32 [32, 32], replicated, may hold values from 0 to 127
Outputs:
- new_entity: float32 [65536, 512], P(('dom', 'rel'))
- new_entity_acc: float32 [65536, 512], P(('dom', 'rel'))
- new_relation: float32 [4096, 512], P('rel')
- new_relation_acc: float32 [4096, 512], P('rel')
The draws below stay inside these ranges and needn't reach their ends.
Inputs may be any that keep to these rules, and one draw needn't show every extreme that they name: `send_rows`: within one owner's list for one receiver the 16 rows are distinct. `relation`: every component has magnitude 0.1 or more.
All inputs are finite; a program needn't handle non-finite values.
Results may differ from the reference program's by a relative error of at most 0.0003.
Values sent between devices are 32-bit elements; how exact they have to be, the bound alone decides.
A program may use at most 64 MiB of HBM per device.

```python
import math
import jax
import jax.numpy as jnp
from jax import lax

RANK = 128
ENT_DEV = 128
REL_DEV = 128
TRIP_DEV = 256
SLOTS = 16
NEG_SLOT = 32
TOUCHED = 512
ENTS = 65536
RELS = 4096
TRIPLES = 131072
N_DOM = 16
N_REL = 32


def draw_relation(key, part):
    key_sign, key_size = jax.random.split(key)
    shape = (REL_DEV * N_REL, 4 * RANK)
    signs = jnp.where(jax.random.bernoulli(key_sign, 0.5, shape), 1.0, -1.0).astype(jnp.float32)
    magnitude = jax.random.uniform(key_size, shape, jnp.float32, 0.25, 1.0)
    return (signs * magnitude).astype(jnp.float32)


def draw_send_rows(key, part):
    shape = (N_DOM * N_REL, N_REL, ENT_DEV)
    scores = jax.random.randint(key, shape, 0, 2 ** 20) * ENT_DEV + lax.broadcasted_iota(jnp.int32, shape, 2)
    order = jnp.argsort(scores, axis=-1, stable=True)
    return order[:, :, :SLOTS].astype(jnp.int32)


def touch_ends(result, key, least, high):
    longest = result.shape.index(max(result.shape))
    spots = []
    for shift in (0, 1):
        where = [jax.random.randint(jax.random.fold_in(key, axis), (), 0, length) for axis, length in enumerate(result.shape)]
        where[longest] = (where[longest] + shift) % result.shape[longest]
        spots.append(tuple(where))
    return result.at[spots[0]].set(least).at[spots[1]].set(high)


def block_scale(key, extent, pieces, smallest, top_value):
    gain, own = 1.0, jax.random.fold_in(key, 6)
    for dim, parts in pieces:
        heights = jnp.exp(jax.random.uniform(jax.random.fold_in(own, dim), (parts,), jnp.float32, smallest / len(pieces), top_value / len(pieces)))
        gain = gain * jnp.repeat(heights, extent[dim] // parts).reshape([-1 if axis == dim else 1 for axis in range(len(extent))])
    return gain


def scatter_about(rng, dims, width, limit, pieces=(), kind=jnp.bfloat16):
    entries = width * jax.random.normal(rng, dims, jnp.float32)
    if pieces:
        entries = entries * block_scale(rng, dims, pieces, -0.22, 0.18)
    return jnp.clip(entries, -limit, limit).astype(kind)


def setup_inputs(seed: int = 0) -> dict:
    arg_keys = jax.random.split(jax.random.key(seed), 11)
    entity = scatter_about(arg_keys[0], (ENTS, 4 * RANK), 0.3, 1.8, ((0, 512),), jnp.float32)
    entity_acc = jnp.clip(jnp.exp(math.log(1.0) - 4.6051702 * jax.random.uniform(arg_keys[1], (ENTS, 4 * RANK), jnp.float32) ** block_scale(arg_keys[1], (ENTS, 4 * RANK), ((0, 512),), -0.2, 0.2)), 0.01, 1.0)
    relation = draw_relation(jax.random.fold_in(arg_keys[10], 71), 0)
    relation_acc = jnp.clip(jnp.exp(math.log(1.0) - 4.6051702 * jax.random.uniform(arg_keys[3], (RELS, 4 * RANK), jnp.float32) ** block_scale(arg_keys[3], (RELS, 4 * RANK), ((0, 32),), -0.2, 0.2)), 0.01, 1.0)
    send_rows = draw_send_rows(jax.random.fold_in(arg_keys[10], 71), 0)
    trip_head = touch_ends(jax.random.randint(arg_keys[5], (TRIPLES,), 0, TOUCHED), jax.random.fold_in(arg_keys[5], 1), 0, TOUCHED - 1).astype(jnp.int32)
    trip_rel = touch_ends(jax.random.randint(arg_keys[6], (TRIPLES,), 0, REL_DEV), jax.random.fold_in(arg_keys[6], 1), 0, REL_DEV - 1).astype(jnp.int32)
    trip_tail = touch_ends(jax.random.randint(arg_keys[7], (TRIPLES,), 0, TOUCHED), jax.random.fold_in(arg_keys[7], 1), 0, TOUCHED - 1).astype(jnp.int32)
    neg_part = jax.random.randint(arg_keys[8], (1,), 0, N_DOM).astype(jnp.int32)
    neg_rows = touch_ends(jax.random.randint(arg_keys[9], (N_REL, NEG_SLOT), 0, ENT_DEV), jax.random.fold_in(arg_keys[9], 1), 0, ENT_DEV - 1).astype(jnp.int32)
    return dict(entity=entity, entity_acc=entity_acc, relation=relation, relation_acc=relation_acc, send_rows=send_rows, trip_head=trip_head, trip_rel=trip_rel, trip_tail=trip_tail, neg_part=neg_part, neg_rows=neg_rows)


step_size = 0.05

def hamilton(left, right):
    left_a, left_b, left_c, left_d = jnp.split(left, 4, axis=-1)
    right_a, right_b, right_c, right_d = jnp.split(right, 4, axis=-1)
    out_a = left_a * right_a - left_b * right_b - left_c * right_c - left_d * right_d
    out_b = left_a * right_b + left_b * right_a + left_c * right_d - left_d * right_c
    out_c = left_a * right_c - left_b * right_d + left_c * right_a + left_d * right_b
    out_d = left_a * right_d + left_b * right_c - left_c * right_b + left_d * right_a
    return jnp.concatenate([out_a, out_b, out_c, out_d], axis=-1)

def unit_rel(relation):
    comp_a, comp_b, comp_c, comp_d = jnp.split(relation, 4, axis=-1)
    magnitude = jnp.sqrt(comp_a * comp_a + comp_b * comp_b + comp_c * comp_c + comp_d * comp_d)
    return relation / jnp.concatenate([magnitude, magnitude, magnitude, magnitude], axis=-1)

def local_loss(touched, relation, negatives, heads, rels, tails):
    unit_rows = unit_rel(relation)
    one_hot = (rels[:, None] == jnp.arange(relation.shape[0])[None, :]).astype(unit_rows.dtype)
    rotation = jnp.dot(one_hot, unit_rows, precision=lax.Precision.HIGHEST)
    query = hamilton(touched[heads], rotation)
    positive = lax.optimization_barrier(jnp.sum(query * touched[tails], axis=-1))
    scores = jnp.einsum('ik,jk->ij', query, negatives, precision=lax.Precision.HIGHEST)
    return jnp.sum(jax.nn.softplus(-positive)) + jnp.sum(jax.nn.softplus(scores)) / negatives.shape[0]

def adagrad(values, history, gradient):
    history_new = history + gradient * gradient
    return (values - step_size * gradient / jnp.sqrt(history_new), history_new)

def reference(entity, entity_acc, relation, relation_acc, send_rows, trip_head, trip_rel, trip_tail, neg_part, neg_rows):
    row_width = entity.shape[1]
    blocks = entity.reshape(N_DOM, N_REL, ENT_DEV, row_width)
    send_lists = send_rows.reshape(N_DOM, N_REL, N_REL, SLOTS)
    rel_blocks = relation.reshape(N_REL, REL_DEV, row_width)
    heads_all = trip_head.reshape(N_DOM * N_REL, TRIP_DEV)
    rels_all = trip_rel.reshape(N_DOM * N_REL, TRIP_DEV)
    tails_all = trip_tail.reshape(N_DOM * N_REL, TRIP_DEV)
    neg_root = neg_part[0]
    sources = jnp.arange(N_REL)[:, None]
    negatives = blocks[neg_root][sources, neg_rows].reshape(NEG_SLOT * N_REL, row_width)

    def device_step(carry, device):
        ent_grad, rel_grad, neg_grad = carry
        dom_here = device // N_REL
        rel_here = device % N_REL
        wanted = send_lists[dom_here][:, rel_here, :]
        touched = blocks[dom_here][sources, wanted].reshape(N_REL * SLOTS, row_width)
        rel_local = rel_blocks[rel_here]
        heads = heads_all[device]
        rels = rels_all[device]
        tails = tails_all[device]

        def scored(touched_in, relation_in, negatives_in):
            return local_loss(touched_in, relation_in, negatives_in, heads, rels, tails)
        loss_value, pullback = jax.vjp(scored, touched, rel_local, negatives)
        grad_rows, grad_rel, grad_neg = pullback(jnp.ones_like(loss_value))
        ent_grad = ent_grad.at[dom_here, sources, wanted].add(grad_rows.reshape(N_REL, SLOTS, row_width))
        rel_grad = rel_grad.at[rel_here].add(grad_rel)
        neg_grad = neg_grad + grad_neg
        return ((ent_grad, rel_grad, neg_grad), None)
    start = (jnp.zeros_like(blocks), jnp.zeros_like(rel_blocks), jnp.zeros_like(negatives))
    (ent_grad, rel_grad, neg_grad), _ = lax.scan(device_step, start, jnp.arange(N_DOM * N_REL))
    ent_grad = ent_grad.at[neg_root, sources, neg_rows].add(neg_grad.reshape(N_REL, NEG_SLOT, row_width))
    new_entity, new_entity_acc = adagrad(entity, entity_acc, ent_grad.reshape(-1, row_width))
    new_relation, new_relation_acc = adagrad(relation, relation_acc, rel_grad.reshape(-1, row_width))
    return (new_entity, new_entity_acc, new_relation, new_relation_acc)
```

```python
import jax
import jax.numpy as jnp
from jax import lax
from jax.experimental import pallas as pl
from jax.experimental.pallas import tpu as pltpu
from jax.sharding import PartitionSpec as P

MESH = pl.DeviceIdType.MESH
F32, BF16 = jnp.float32, jnp.bfloat16
step_size = 0.05

N_DOM, N_REL = 16, 32
NY, NX = 8, 4
ZX = 32
ENT, RELS, TRIP, SLOTS, NEG, WIDTH = 128, 128, 256, 16, 32, 512
TILE = (8, 128)
NEGS = NEG * N_REL

NN = (((1,), (0,)), ((), ()))
TN = (((0,), (0,)), ((), ()))
NT = (((1,), (1,)), ((), ()))


def mm(a, b, dims):
    return lax.dot_general(a, b, dims, preferred_element_type=F32)


def halves(v):
    hi = v.astype(BF16)
    return hi, (v - hi.astype(F32)).astype(BF16)


def select(one_hot, v, dims):
    hi, lo = halves(v)
    return mm(one_hot, hi, dims) + mm(one_hot, lo, dims)


def mm3(a, b, dims):
    return mm(a[0], b[0], dims) + (mm(a[0], b[1], dims) + mm(a[1], b[0], dims))


def hot(rows, index_row):
    n = index_row.shape[1]
    at = lax.broadcasted_iota(jnp.int32, (rows, n), 0)
    return jnp.where(at == index_row, 1.0, 0.0).astype(BF16)


def rcopy(src, dst, ssem, rsem, dev):
    return pltpu.make_async_remote_copy(
        src_ref=src, dst_ref=dst, send_sem=ssem, recv_sem=rsem, device_id=dev, device_id_type=MESH
    )


def quarter(v):
    return v[:, 0:128], v[:, 128:256], v[:, 256:384], v[:, 384:512]


def adagrad(values, history, gradient):
    history_new = history + gradient * gradient
    return values - step_size * gradient / jnp.sqrt(history_new), history_new


def kernel(
    entity, entity_acc, relation, relation_acc, send_row, ends_row, rels_row, neg_rows, neg_part,
    new_e, new_ea, new_r, new_ra,
    send_buf, recv, neg_src, s1_recv, nbuf, hot_ends, ends, rot, query, dq, dends,
    gall, xrecv, ring, rp, rm, zx_recv, relx, tile_out, t_recv, rel_full, gt, ret,
    a_s, a_r, b_s, b_r, s1_s, s1_r, s2_s, s2_r, yp_s, yp_r, ym_s, ym_r, sib_s, sib_r, x_s, x_r,
    rp_s, rp_r, rm_s, rm_r, z_s, z_r, rx_s, rx_r, t_s, t_r, ra_s, ra_r,
):
    dom, rel = lax.axis_index("dom"), lax.axis_index("rel")
    zh, y = lax.div(dom, NY), lax.rem(dom, NY)
    zx_low, core = lax.div(rel, 2), lax.rem(rel, 2)
    zi = zh * 16 + zx_low
    root = neg_part[0]
    up, down = lax.rem(y + 1, NY), lax.rem(y + NY - 1, NY)
    up_dev, down_dev = {"dom": zh * NY + up}, {"dom": zh * NY + down}
    sib_dev = {"rel": zx_low * 2 + (1 - core)}

    def zx_dev(p):
        return {"dom": lax.div(p, 16) * NY + y, "rel": lax.rem(p, 16) * 2 + core}

    barrier = pltpu.get_barrier_semaphore()

    @pl.loop(1, N_DOM)
    def _(k):
        pl.semaphore_signal(
            barrier, inc=1, device_id={"dom": lax.rem(dom + k, N_DOM)}, device_id_type=MESH
        )

    @pl.loop(1, N_REL)
    def _(k):
        pl.semaphore_signal(
            barrier, inc=1, device_id={"rel": lax.rem(rel + k, N_REL)}, device_id_type=MESH
        )

    @pl.loop(1, 16)
    def _(k):
        p = (1 - zh) * 16 + lax.rem(zx_low + k, 16)
        pl.semaphore_signal(barrier, inc=1, device_id=zx_dev(p), device_id_type=MESH)

    ent = entity[...]
    neg_hot = hot(ENT, neg_rows[pl.ds(rel, 1), :])
    own = select(neg_hot, ent, TN)
    for g in range(4):
        for w in range(4):
            neg_src[g * 4 + w] = own[g * 8 : g * 8 + 8, w * 128 : w * 128 + 128]
    send_hot = hot(ENT, send_row[...])
    send_buf[...] = select(send_hot, ent, TN).reshape(N_REL, SLOTS, WIDTH)

    pl.semaphore_wait(barrier, (N_DOM - 1) + (N_REL - 1) + 15)

    @pl.loop(1, N_DOM)
    def _(k):
        p = lax.rem(dom + k, N_DOM)
        rcopy(neg_src.at[p], s1_recv.at[dom], s1_s.at[k], s1_r.at[dom], {"dom": p}).start()

    def exchange(src, dst, ssem, rsem, k):
        p = lax.rem(rel + k, N_REL)
        rcopy(src.at[p], dst.at[rel], ssem.at[k], rsem.at[rel], {"rel": p}).start()

    @pl.loop(16, N_REL)
    def _(k):
        exchange(send_buf, recv, a_s, a_r, k)

    s1_recv[dom] = neg_src[dom]
    recv[rel] = send_buf[rel]

    @pl.loop(1, N_DOM)
    def _(k):
        p = lax.rem(dom + k, N_DOM)
        rcopy(neg_src.at[p], s1_recv.at[p], s1_s.at[k], s1_r.at[p], {"dom": p}).wait_recv()

    mine = core * NY + y
    nbuf[mine, zi] = s1_recv[root]

    @pl.loop(1, ZX)
    def _(k):
        p = lax.rem(zi + k, ZX)
        here = nbuf.at[mine, zi]
        rcopy(here, here, s2_s.at[k], s2_r.at[zi], zx_dev(p)).start()

    @pl.loop(1, 16)
    def _(k):
        exchange(send_buf, recv, a_s, a_r, k)

    @pl.loop(1, ZX)
    def _(k):
        p = lax.rem(zi + k, ZX)
        there = nbuf.at[mine, p]
        rcopy(there, there, s2_s.at[k], s2_r.at[p], zx_dev(p)).wait_recv()

    def block(yy):
        return nbuf.at[core * NY + lax.rem(yy + 2 * NY, NY)]

    def part(yy, lo):
        return nbuf.at[core * NY + lax.rem(yy + 2 * NY, NY), pl.ds(lo, ZX // 2)]

    def pass_up(ref, n):
        return rcopy(ref, ref, yp_s.at[n], yp_r.at[n], up_dev)

    def pass_down(ref, n):
        return rcopy(ref, ref, ym_s.at[n], ym_r.at[n], down_dev)

    def to_sib(ref, n):
        return rcopy(ref, ref, sib_s.at[n], sib_r.at[n], sib_dev)

    sent = [pass_up(block(y), 0), pass_down(block(y), 0), to_sib(block(y), 0)]
    for c in sent:
        c.start()
    for n in (1, 2):
        pass_up(block(y - n), n - 1).wait_recv()
        nxt = [pass_up(block(y - n), n), to_sib(block(y - n), 2 * n - 1)]
        for c in nxt:
            c.start()
        sent += nxt
        pass_down(block(y + n), n - 1).wait_recv()
        nxt = [pass_down(block(y + n), n), to_sib(block(y + n), 2 * n)]
        for c in nxt:
            c.start()
        sent += nxt
    half = ZX // 2
    pass_up(block(y - 3), 2).wait_recv()
    nxt = [pass_up(part(y - 3, 0), 3), to_sib(block(y - 3), 5)]
    for c in nxt:
        c.start()
    sent += nxt
    pass_down(block(y + 3), 2).wait_recv()
    nxt = [pass_down(part(y + 3, half), 3), to_sib(block(y + 3), 6)]
    for c in nxt:
        c.start()
    sent += nxt

    @pl.loop(1, N_REL)
    def _(k):
        p = lax.rem(rel + k, N_REL)
        rcopy(send_buf.at[p], recv.at[p], a_s.at[k], a_r.at[p], {"rel": p}).wait_recv()

    hot_ends[...] = hot(N_REL * SLOTS, ends_row[...])
    ends[...] = select(hot_ends[...], recv[...].reshape(N_REL * SLOTS, WIDTH), TN)
    rel_hot = hot(RELS, rels_row[...])
    ra, rb, rc, rd = quarter(relation[...])
    inv = 1.0 / jnp.sqrt(ra * ra + rb * rb + rc * rc + rd * rd)
    unit = jnp.concatenate([ra * inv, rb * inv, rc * inv, rd * inv], axis=1)
    rot[...] = select(rel_hot, unit, TN)
    ha, hb, hc, hd = quarter(ends[pl.ds(0, TRIP), :])
    ua, ub, uc, ud = quarter(rot[...])
    qa = ha * ua - hb * ub - hc * uc - hd * ud
    qb = ha * ub + hb * ua + hc * ud - hd * uc
    qc = ha * uc - hb * ud + hc * ua + hd * ub
    qd = ha * ud + hb * uc - hc * ub + hd * ua
    query[...] = jnp.concatenate([qa, qb, qc, qd], axis=1)
    tails = ends[pl.ds(TRIP, TRIP), :]
    positive = jnp.sum(query[...] * tails, axis=1, keepdims=True)
    pull = -1.0 / (1.0 + jnp.exp(positive))
    dq[...] = pull * tails
    dends[pl.ds(TRIP, TRIP), :] = pull * query[...]

    pass_up(part(y - 4, 0), 3).wait_recv()
    nxt = [to_sib(part(y - 4, 0), 7)]
    nxt[0].start()
    sent += nxt
    pass_down(part(y + 4, half), 3).wait_recv()
    nxt = [to_sib(part(y + 4, half), 8)]
    nxt[0].start()
    sent += nxt

    def sib_block(yy):
        return nbuf.at[(1 - core) * NY + lax.rem(yy + 2 * NY, NY)]

    def sib_part(yy, lo):
        return nbuf.at[(1 - core) * NY + lax.rem(yy + 2 * NY, NY), pl.ds(lo, half)]

    to_sib(sib_block(y), 0).wait_recv()
    for n in (1, 2, 3):
        to_sib(sib_block(y - n), 2 * n - 1).wait_recv()
        to_sib(sib_block(y + n), 2 * n).wait_recv()
    to_sib(sib_part(y - 4, 0), 7).wait_recv()
    to_sib(sib_part(y + 4, half), 8).wait_recv()

    @pl.loop(0, 4)
    def _(b):
        q = halves(query[...])
        n = halves(
            jnp.concatenate(
                [nbuf[b * 4 + w].reshape(ZX * 8, 128) for w in range(4)], axis=1
            )
        )
        s = mm3(q, n, NT)
        p = halves((1.0 / NEGS) / (1.0 + jnp.exp(-s)))
        dq[...] += mm3(p, n, NN)
        dn = mm3(p, q, TN)
        for w in range(4):
            gall[b * 4 + w] = dn[:, w * 128 : w * 128 + 128].reshape(ZX, 8, 128)

    swap = rcopy(gall.at[pl.ds((1 - core) * NY, NY)], xrecv, x_s, x_r, sib_dev)
    swap.start()
    sent.append(swap)

    ga, gb, gc, gd = quarter(dq[...])
    ha, hb, hc, hd = quarter(ends[pl.ds(0, TRIP), :])
    ua, ub, uc, ud = quarter(rot[...])
    dha = ga * ua + gb * ub + gc * uc + gd * ud
    dhb = gb * ua - ga * ub - gc * ud + gd * uc
    dhc = gb * ud - ga * uc + gc * ua - gd * ub
    dhd = gc * ub - ga * ud - gb * uc + gd * ua
    dends[pl.ds(0, TRIP), :] = jnp.concatenate([dha, dhb, dhc, dhd], axis=1)
    gt[...] = select(hot_ends[...], dends[...], NN).reshape(N_REL, SLOTS, WIDTH)

    @pl.loop(16, N_REL)
    def _(k):
        exchange(gt, ret, b_s, b_r, k)

    @pl.loop(1, 16)
    def _(k):
        exchange(gt, ret, b_s, b_r, k)

    ret[rel] = gt[rel]
    dua = ga * ha + gb * hb + gc * hc + gd * hd
    dub = gb * ha - ga * hb + gc * hd - gd * hc
    duc = gc * ha - ga * hc - gb * hd + gd * hb
    dud = gb * hc - ga * hd - gc * hb + gd * ha
    rel_hot = hot(RELS, rels_row[...])
    du = select(rel_hot, jnp.concatenate([dua, dub, duc, dud], axis=1), NN)
    ra, rb, rc, rd = quarter(relation[...])
    inv = 1.0 / jnp.sqrt(ra * ra + rb * rb + rc * rc + rd * rd)
    va, vb, vc, vd = ra * inv, rb * inv, rc * inv, rd * inv
    da, db, dc, dd = quarter(du)
    along = da * va + db * vb + dc * vc + dd * vd
    parts = [(g - v * along) * inv for g, v in ((da, va), (db, vb), (dc, vc), (dd, vd))]
    for yy in range(NY):
        for g in range(2):
            for w in range(4):
                at = yy * 16 + g * 8
                ring[yy, ZX + g * 4 + w] = parts[w][at : at + 8, :]

    rcopy(gall.at[pl.ds(core * NY, NY)], xrecv, x_s, x_r, sib_dev).wait_recv()

    @pl.loop(0, NY)
    def _(k):
        ring[k, pl.ds(0, ZX)] = gall[core * NY + k] + xrecv[k]

    def chunk(yy, lo, n):
        return ring.at[lax.rem(yy + 2 * NY, NY), pl.ds(lo, n)]

    def add_up(yy, lo, n, got):
        i = lax.rem(yy + 2 * NY, NY)
        ring[i, pl.ds(lo, n)] = ring[i, pl.ds(lo, n)] + got[pl.ds(lo, n)]

    def sum_up(yy, lo, n, s):
        return rcopy(chunk(yy, lo, n), rp.at[s, pl.ds(lo, n)], rp_s.at[s], rp_r.at[s], up_dev)

    def sum_down(yy, lo, n, s):
        return rcopy(chunk(yy, lo, n), rm.at[s, pl.ds(lo, n)], rm_s.at[s], rm_r.at[s], down_dev)

    nxt = [sum_up(y + 4, 0, 20, 0), sum_down(y - 4, 20, 20, 0)]
    for c in nxt:
        c.start()
    sent += nxt
    for s in (1, 2, 3):
        lo_u, n_u, lo_d, n_d = (0, 20, 20, 20) if s == 1 else (0, 40, 0, 40)
        sum_up(y + 4 - s, lo_u, n_u, s - 1).wait_recv()
        add_up(y + 4 - s, lo_u, n_u, rp.at[s - 1])
        c = sum_up(y + 4 - s, 0, 40, s)
        c.start()
        sent.append(c)
        sum_down(y - 4 + s, lo_d, n_d, s - 1).wait_recv()
        add_up(y - 4 + s, lo_d, n_d, rm.at[s - 1])
        c = sum_down(y - 4 + s, 0, 40, s)
        c.start()
        sent.append(c)
    sum_up(y, 0, 40, 3).wait_recv()
    sum_down(y, 0, 40, 3).wait_recv()
    ring[y] = ring[y] + (rp[3] + rm[3])

    far = {"dom": (1 - zh) * NY + y}
    cross = rcopy(ring.at[y, pl.ds(ZX, 8)], relx, rx_s, rx_r, far)
    cross.start()
    sent.append(cross)

    @pl.loop(1, ZX)
    def _(k):
        p = lax.rem(zi + k, ZX)
        rcopy(ring.at[y, p], zx_recv.at[zi], z_s.at[k], z_r.at[zi], zx_dev(p)).start()

    zx_recv[zi] = ring[y, zi]

    @pl.loop(1, ZX)
    def _(k):
        p = lax.rem(zi + k, ZX)
        rcopy(ring.at[y, p], zx_recv.at[p], z_s.at[k], z_r.at[p], zx_dev(p)).wait_recv()

    tile_out[...] = jnp.sum(zx_recv[...], axis=0)

    @pl.loop(1, N_DOM)
    def _(k):
        p = lax.rem(dom + k, N_DOM)
        rcopy(tile_out, t_recv.at[dom], t_s.at[k], t_r.at[dom], {"dom": p}).start()

    t_recv[dom] = tile_out[...]
    cross.wait_recv()
    rel_full[y] = ring[y, pl.ds(ZX, 8)] + relx[...]

    @pl.loop(1, NY)
    def _(k):
        to = {"dom": zh * NY + lax.rem(y + k, NY)}
        rcopy(rel_full.at[y], rel_full.at[y], ra_s.at[k], ra_r.at[y], to).start()

    @pl.loop(1, N_REL)
    def _(k):
        p = lax.rem(rel + k, N_REL)
        rcopy(gt.at[p], ret.at[p], b_s.at[k], b_r.at[p], {"rel": p}).wait_recv()

    send_hot = hot(ENT, send_row[...])
    grad = select(send_hot, ret[...].reshape(N_REL * SLOTS, WIDTH), NN)

    @pl.loop(1, N_DOM)
    def _(k):
        p = lax.rem(dom + k, N_DOM)
        rcopy(tile_out, t_recv.at[p], t_s.at[k], t_r.at[p], {"dom": p}).wait_recv()

    total = jnp.concatenate(
        [
            jnp.concatenate([t_recv[g * 4 + w] for w in range(4)], axis=1)
            for g in range(4)
        ],
        axis=0,
    )
    owner = jnp.where(dom == root, 1.0, 0.0).astype(F32)
    neg_hot = hot(ENT, neg_rows[pl.ds(rel, 1), :])
    grad = grad + owner * select(neg_hot, total, NN)
    e, ea = adagrad(entity[...], entity_acc[...], grad)
    new_e[...] = e
    new_ea[...] = ea

    @pl.loop(1, NY)
    def _(k):
        i = lax.rem(y + k, NY)
        there = rel_full.at[i]
        rcopy(there, there, ra_s.at[k], ra_r.at[i], {"dom": zh * NY + i}).wait_recv()

    for w in range(4):
        cols = pl.ds(w * 128, 128)
        g = jnp.concatenate(
            [rel_full[yy, gg * 4 + w] for yy in range(NY) for gg in range(2)], axis=0
        )
        r, racc = adagrad(relation[:, cols], relation_acc[:, cols], g)
        new_r[:, cols] = r
        new_ra[:, cols] = racc

    for c in sent:
        c.wait_send()

    @pl.loop(1, N_DOM)
    def _(k):
        p = lax.rem(dom + k, N_DOM)
        rcopy(neg_src.at[p], s1_recv.at[dom], s1_s.at[k], s1_r.at[dom], {"dom": p}).wait_send()
        rcopy(tile_out, t_recv.at[dom], t_s.at[k], t_r.at[dom], {"dom": p}).wait_send()

    @pl.loop(1, N_REL)
    def _(k):
        p = lax.rem(rel + k, N_REL)
        rcopy(send_buf.at[p], recv.at[rel], a_s.at[k], a_r.at[rel], {"rel": p}).wait_send()
        rcopy(gt.at[p], ret.at[rel], b_s.at[k], b_r.at[rel], {"rel": p}).wait_send()

    @pl.loop(1, ZX)
    def _(k):
        p = lax.rem(zi + k, ZX)
        here = nbuf.at[mine, zi]
        rcopy(here, here, s2_s.at[k], s2_r.at[zi], zx_dev(p)).wait_send()
        rcopy(ring.at[y, p], zx_recv.at[zi], z_s.at[k], z_r.at[zi], zx_dev(p)).wait_send()

    @pl.loop(1, NY)
    def _(k):
        to = {"dom": zh * NY + lax.rem(y + k, NY)}
        rcopy(rel_full.at[y], rel_full.at[y], ra_s.at[k], ra_r.at[y], to).wait_send()


def shards(
    entity, entity_acc, relation, relation_acc, send_rows, trip_head, trip_rel, trip_tail, neg_part, neg_rows,
):
    send_row = send_rows.reshape(1, N_REL * SLOTS)
    ends_row = jnp.concatenate([trip_head, trip_tail]).reshape(1, 2 * TRIP)
    rels_row = trip_rel.reshape(1, TRIP)
    vmem = pl.BlockSpec(memory_space=pltpu.VMEM)
    smem = pl.BlockSpec(memory_space=pltpu.SMEM)
    dma = pltpu.SemaphoreType.DMA
    rows = jax.ShapeDtypeStruct((ENT, WIDTH), F32)
    return pl.pallas_call(
        kernel,
        out_shape=(rows, rows, rows, rows),
        in_specs=[vmem] * 8 + [smem],
        out_specs=(vmem,) * 4,
        scratch_shapes=[
            pltpu.VMEM((N_REL, SLOTS, WIDTH), F32),
            pltpu.VMEM((N_REL, SLOTS, WIDTH), F32),
            pltpu.VMEM((N_DOM, *TILE), F32),
            pltpu.VMEM((N_DOM, *TILE), F32),
            pltpu.VMEM((2 * NY, ZX, *TILE), F32),
            pltpu.VMEM((N_REL * SLOTS, 2 * TRIP), BF16),
            pltpu.VMEM((2 * TRIP, WIDTH), F32),
            pltpu.VMEM((TRIP, WIDTH), F32),
            pltpu.VMEM((TRIP, WIDTH), F32),
            pltpu.VMEM((TRIP, WIDTH), F32),
            pltpu.VMEM((2 * TRIP, WIDTH), F32),
            pltpu.VMEM((2 * NY, ZX, *TILE), F32),
            pltpu.VMEM((NY, ZX, *TILE), F32),
            pltpu.VMEM((NY, ZX + 8, *TILE), F32),
            pltpu.VMEM((4, ZX + 8, *TILE), F32),
            pltpu.VMEM((4, ZX + 8, *TILE), F32),
            pltpu.VMEM((ZX, *TILE), F32),
            pltpu.VMEM((8, *TILE), F32),
            pltpu.VMEM(TILE, F32),
            pltpu.VMEM((N_DOM, *TILE), F32),
            pltpu.VMEM((NY, 8, *TILE), F32),
            pltpu.VMEM((N_REL, SLOTS, WIDTH), F32),
            pltpu.VMEM((N_REL, SLOTS, WIDTH), F32),
            dma((N_REL,)), dma((N_REL,)), dma((N_REL,)), dma((N_REL,)),
            dma((N_DOM,)), dma((N_DOM,)), dma((ZX,)), dma((ZX,)),
            dma((4,)), dma((4,)), dma((4,)), dma((4,)),
            dma((9,)), dma((9,)), dma, dma,
            dma((4,)), dma((4,)), dma((4,)), dma((4,)),
            dma((ZX,)), dma((ZX,)), dma, dma,
            dma((N_DOM,)), dma((N_DOM,)), dma((NY,)), dma((NY,)),
        ],
        compiler_params=pltpu.CompilerParams(
            collective_id=0, has_side_effects=True, vmem_limit_bytes=56 << 20
        ),
        name="step",
    )(entity, entity_acc, relation, relation_acc, send_row, ends_row, rels_row, neg_rows, neg_part)


def solution(mesh):
    both = ("dom", "rel")
    in_specs = (
        P(both, None), P(both, None), P("rel", None), P("rel", None), P(both, None, None),
        P(both), P(both), P(both), P(), P(),
    )
    out_specs = (P(both, None), P(both, None), P("rel", None), P("rel", None))
    return jax.shard_map(shards, mesh=mesh, in_specs=in_specs, out_specs=out_specs, check_vma=False)
```

```python
import jax
import jax.numpy as jnp
from jax import lax
from jax.experimental import pallas as pl
from jax.experimental.pallas import tpu as pltpu
from jax.sharding import PartitionSpec as P

MESH = pl.DeviceIdType.MESH
F32, BF16 = jnp.float32, jnp.bfloat16
step_size = 0.05

N_DOM, N_REL = 16, 32
NY, NX = 8, 4
ZX = 32
ENT, RELS, TRIP, SLOTS, NEG, WIDTH = 128, 128, 256, 16, 32, 512
TILE = (8, 128)
NEGS = NEG * N_REL
FIRST = 24
HALF = ZX // 2
CUT = 20

NN = (((1,), (0,)), ((), ()))
TN = (((0,), (0,)), ((), ()))
NT = (((1,), (1,)), ((), ()))


def mm(a, b, dims):
    return lax.dot_general(a, b, dims, preferred_element_type=F32)


def halves(v):
    hi = v.astype(BF16)
    return hi, (v - hi.astype(F32)).astype(BF16)


def select(one_hot, v, dims):
    hi, lo = halves(v)
    return mm(one_hot, hi, dims) + mm(one_hot, lo, dims)


def mm3(a, b, dims):
    return mm(a[0], b[0], dims) + (mm(a[0], b[1], dims) + mm(a[1], b[0], dims))


def hot(rows, index_row):
    n = index_row.shape[1]
    at = lax.broadcasted_iota(jnp.int32, (rows, n), 0)
    return jnp.where(at == index_row, 1.0, 0.0).astype(BF16)


def slot_row(send_t):
    n = N_REL * SLOTS
    at = lax.broadcasted_iota(jnp.int32, (N_REL, n), 1)
    spread = lax.div(at, SLOTS) == lax.broadcasted_iota(jnp.int32, (N_REL, n), 0)
    full = mm(
        send_t[...].astype(F32).astype(BF16), jnp.where(spread, 1.0, 0.0).astype(BF16), NN
    )
    slot = lax.rem(lax.broadcasted_iota(jnp.int32, (SLOTS, n), 1), SLOTS)
    keep = slot == lax.broadcasted_iota(jnp.int32, (SLOTS, n), 0)
    return jnp.sum(jnp.where(keep, full, 0.0), axis=0, keepdims=True).astype(jnp.int32)


def rcopy(src, dst, ssem, rsem, dev):
    return pltpu.make_async_remote_copy(
        src_ref=src, dst_ref=dst, send_sem=ssem, recv_sem=rsem, device_id=dev, device_id_type=MESH
    )


def quarter(v):
    return v[:, 0:128], v[:, 128:256], v[:, 256:384], v[:, 384:512]


def adagrad(values, history, gradient):
    history_new = history + gradient * gradient
    return values - step_size * gradient / jnp.sqrt(history_new), history_new


def kernel(
    entity_h, relation_h, send_h, head_h, tail_h, rels_h, neg_h, part_h,
    grad_e, grad_r,
    entity, relation, send_t, head_row, tail_row, rels_row, neg_rows, neg_part,
    send_buf, recv, neg_src, s1_recv, nbuf, hot_ends, ends, rot, query, dq, dends,
    gall, xrecv, ring, rp, rm, zx_recv, relx, tile_out, t_recv, rel_full, gt, ret,
    in_s, a_s, a_r, b_s, b_r, s1_s, s1_r, s2_s, s2_r, yp_s, yp_r, ym_s, ym_r, sib_s, sib_r, x_s, x_r,
    rp_s, rp_r, rm_s, rm_r, z_s, z_r, rx_s, rx_r, t_s, t_r, ra_s, ra_r,
):
    loads = [
        pltpu.make_async_copy(h, v, in_s.at[n])
        for n, (h, v) in enumerate(
            (
                (entity_h, entity), (neg_h, neg_rows), (send_h, send_t), (part_h, neg_part),
                (head_h, head_row), (tail_h, tail_row), (rels_h, rels_row), (relation_h, relation),
            )
        )
    ]
    for c in loads:
        c.start()
    dom, rel = lax.axis_index("dom"), lax.axis_index("rel")
    zh, y = lax.div(dom, NY), lax.rem(dom, NY)
    zx_low, core = lax.div(rel, 2), lax.rem(rel, 2)
    zi = zh * 16 + zx_low
    up, down = lax.rem(y + 1, NY), lax.rem(y + NY - 1, NY)
    up_dev, down_dev = {"dom": zh * NY + up}, {"dom": zh * NY + down}
    sib_dev = {"rel": zx_low * 2 + (1 - core)}

    def zx_dev(p):
        return {"dom": lax.div(p, 16) * NY + y, "rel": lax.rem(p, 16) * 2 + core}

    barrier = pltpu.get_barrier_semaphore()

    @pl.loop(1, N_DOM)
    def _(k):
        pl.semaphore_signal(
            barrier, inc=1, device_id={"dom": lax.rem(dom + k, N_DOM)}, device_id_type=MESH
        )

    @pl.loop(1, N_REL)
    def _(k):
        pl.semaphore_signal(
            barrier, inc=1, device_id={"rel": lax.rem(rel + k, N_REL)}, device_id_type=MESH
        )

    @pl.loop(1, 16)
    def _(k):
        p = (1 - zh) * 16 + lax.rem(zx_low + k, 16)
        pl.semaphore_signal(barrier, inc=1, device_id=zx_dev(p), device_id_type=MESH)

    for c in loads[:4]:
        c.wait()
    ent = halves(entity[...])
    neg_hot = hot(ENT, neg_rows[pl.ds(rel, 1), :])
    own = mm(neg_hot, ent[0], TN) + mm(neg_hot, ent[1], TN)
    for g in range(4):
        for w in range(4):
            neg_src[g * 4 + w] = own[g * 8 : g * 8 + 8, w * 128 : w * 128 + 128]
    send_hot = hot(ENT, slot_row(send_t))
    rows = mm(send_hot, ent[0], TN) + mm(send_hot, ent[1], TN)
    send_buf[...] = rows.reshape(N_REL, SLOTS, WIDTH)
    for c in loads[4:]:
        c.wait()
    is_root = lax.broadcasted_iota(jnp.int32, (N_DOM, 1, 1), 0) == neg_part[...].reshape(1, 1, 1)

    pl.semaphore_wait(barrier, (N_DOM - 1) + (N_REL - 1) + 15)

    @pl.loop(1, N_DOM)
    def _(k):
        p = lax.rem(dom + k, N_DOM)
        rcopy(neg_src.at[p], s1_recv.at[dom], s1_s.at[k], s1_r.at[dom], {"dom": p}).start()

    def exchange(src, dst, ssem, rsem, k):
        p = lax.rem(rel + k, N_REL)
        rcopy(src.at[p], dst.at[rel], ssem.at[k], rsem.at[rel], {"rel": p}).start()

    @pl.loop(FIRST, N_REL)
    def _(k):
        exchange(send_buf, recv, a_s, a_r, k)

    s1_recv[dom] = neg_src[dom]
    recv[rel] = send_buf[rel]

    @pl.loop(1, N_DOM)
    def _(k):
        p = lax.rem(dom + k, N_DOM)
        rcopy(neg_src.at[p], s1_recv.at[p], s1_s.at[k], s1_r.at[p], {"dom": p}).wait_recv()

    mine = core * NY + y
    nbuf[mine, zi] = jnp.sum(jnp.where(is_root, s1_recv[...], 0.0), axis=0)

    @pl.loop(1, ZX)
    def _(k):
        p = lax.rem(zi + k, ZX)
        here = nbuf.at[mine, zi]
        rcopy(here, here, s2_s.at[k], s2_r.at[zi], zx_dev(p)).start()

    @pl.loop(1, FIRST)
    def _(k):
        exchange(send_buf, recv, a_s, a_r, k)

    @pl.loop(1, ZX)
    def _(k):
        p = lax.rem(zi + k, ZX)
        there = nbuf.at[mine, p]
        rcopy(there, there, s2_s.at[k], s2_r.at[p], zx_dev(p)).wait_recv()

    def part(core_of, yy, h):
        return nbuf.at[core_of * NY + lax.rem(yy + 2 * NY, NY), pl.ds(h * HALF, HALF)]

    def pass_up(yy, h, n):
        ref = part(core, yy, h)
        return rcopy(ref, ref, yp_s.at[2 * n + h], yp_r.at[2 * n + h], up_dev)

    def pass_down(yy, h, n):
        ref = part(core, yy, h)
        return rcopy(ref, ref, ym_s.at[2 * n + h], ym_r.at[2 * n + h], down_dev)

    def to_sib(core_of, off, h):
        ref = part(core_of, y + off, h)
        at = 2 * (off + 4) + h
        return rcopy(ref, ref, sib_s.at[at], sib_r.at[at], sib_dev)

    sent = []

    def go(c):
        c.start()
        sent.append(c)

    for h in (0, 1):
        go(pass_up(y, h, 0))
        go(pass_down(y, h, 0))
    for h in (0, 1):
        go(to_sib(core, 0, h))
    for n in (1, 2, 3):
        for h in (0, 1):
            pass_up(y - n, h, n - 1).wait_recv()
            if n < 3 or h == 0:
                go(pass_up(y - n, h, n))
            go(to_sib(core, -n, h))
            pass_down(y + n, h, n - 1).wait_recv()
            if n < 3 or h == 1:
                go(pass_down(y + n, h, n))
            go(to_sib(core, n, h))

    @pl.loop(1, N_REL)
    def _(k):
        p = lax.rem(rel + k, N_REL)
        rcopy(send_buf.at[p], recv.at[p], a_s.at[k], a_r.at[p], {"rel": p}).wait_recv()

    hot_ends[:, pl.ds(0, TRIP)] = hot(N_REL * SLOTS, head_row[...])
    hot_ends[:, pl.ds(TRIP, TRIP)] = hot(N_REL * SLOTS, tail_row[...])
    ends[...] = select(hot_ends[...], recv[...].reshape(N_REL * SLOTS, WIDTH), TN)
    rel_hot = hot(RELS, rels_row[...])
    ra, rb, rc, rd = quarter(relation[...])
    inv = 1.0 / jnp.sqrt(ra * ra + rb * rb + rc * rc + rd * rd)
    unit = jnp.concatenate([ra * inv, rb * inv, rc * inv, rd * inv], axis=1)
    rot[...] = select(rel_hot, unit, TN)
    ha, hb, hc, hd = quarter(ends[pl.ds(0, TRIP), :])
    ua, ub, uc, ud = quarter(rot[...])
    qa = ha * ua - hb * ub - hc * uc - hd * ud
    qb = ha * ub + hb * ua + hc * ud - hd * uc
    qc = ha * uc - hb * ud + hc * ua + hd * ub
    qd = ha * ud + hb * uc - hc * ub + hd * ua
    query[...] = jnp.concatenate([qa, qb, qc, qd], axis=1)
    tails = ends[pl.ds(TRIP, TRIP), :]
    positive = jnp.sum(query[...] * tails, axis=1, keepdims=True)
    pull = -1.0 / (1.0 + jnp.exp(positive))
    dq[...] = pull * tails
    dends[pl.ds(TRIP, TRIP), :] = pull * query[...]

    pass_up(y - 4, 0, 3).wait_recv()
    go(to_sib(core, -4, 0))
    pass_down(y + 4, 1, 3).wait_recv()
    go(to_sib(core, -4, 1))
    for off in (0, -1, 1, -2, 2, -3, 3, -4):
        for h in (0, 1):
            to_sib(1 - core, off, h).wait_recv()

    def score(b):
        q = halves(query[...])
        n = halves(
            jnp.concatenate(
                [nbuf[b * 4 + w].reshape(ZX * 8, 128) for w in range(4)], axis=1
            )
        )
        s = mm3(q, n, NT)
        p = halves((1.0 / NEGS) / (1.0 + jnp.exp(-s)))
        dq[...] += mm3(p, n, NN)
        dn = mm3(p, q, TN)
        for w in range(4):
            gall[b * 4 + w] = dn[:, w * 128 : w * 128 + 128].reshape(ZX, 8, 128)

    swap = rcopy(gall.at[pl.ds((1 - core) * NY, NY)], xrecv, x_s, x_r, sib_dev)

    @pl.loop(0, 2)
    def _(b):
        score((1 - core) * 2 + b)

    go(swap)

    @pl.loop(0, 2)
    def _(b):
        score(core * 2 + b)

    ga, gb, gc, gd = quarter(dq[...])
    ha, hb, hc, hd = quarter(ends[pl.ds(0, TRIP), :])
    ua, ub, uc, ud = quarter(rot[...])
    dua = ga * ha + gb * hb + gc * hc + gd * hd
    dub = gb * ha - ga * hb + gc * hd - gd * hc
    duc = gc * ha - ga * hc - gb * hd + gd * hb
    dud = gb * hc - ga * hd - gc * hb + gd * ha
    rel_hot = hot(RELS, rels_row[...])
    du = select(rel_hot, jnp.concatenate([dua, dub, duc, dud], axis=1), NN)
    ra, rb, rc, rd = quarter(relation[...])
    inv = 1.0 / jnp.sqrt(ra * ra + rb * rb + rc * rc + rd * rd)
    va, vb, vc, vd = ra * inv, rb * inv, rc * inv, rd * inv
    da, db, dc, dd = quarter(du)
    along = da * va + db * vb + dc * vc + dd * vd
    parts = [(g - v * along) * inv for g, v in ((da, va), (db, vb), (dc, vc), (dd, vd))]
    for yy in range(NY):
        for g in range(2):
            for w in range(4):
                at = yy * 16 + g * 8
                ring[yy, ZX + g * 4 + w] = parts[w][at : at + 8, :]

    rcopy(gall.at[pl.ds(core * NY, NY)], xrecv, x_s, x_r, sib_dev).wait_recv()

    @pl.loop(0, NY)
    def _(k):
        ring[k, pl.ds(0, ZX)] = gall[core * NY + k] + xrecv[k]

    def chunk(yy, h):
        return ring.at[lax.rem(yy + 2 * NY, NY), pl.ds(h * CUT, CUT)]

    def take(yy, h, got, n):
        i = lax.rem(yy + 2 * NY, NY)
        cols = pl.ds(h * CUT, CUT)
        ring[i, cols] = ring[i, cols] + got[n, cols]

    def sum_up(yy, h, n):
        at = 2 * n + h
        dst = rp.at[n, pl.ds(h * CUT, CUT)]
        return rcopy(chunk(yy, h), dst, rp_s.at[at], rp_r.at[at], up_dev)

    def sum_down(yy, h, n):
        at = 2 * n + h
        dst = rm.at[n, pl.ds(h * CUT, CUT)]
        return rcopy(chunk(yy, h), dst, rm_s.at[at], rm_r.at[at], down_dev)

    go(sum_up(y + 4, 0, 0))
    go(sum_down(y - 4, 1, 0))
    go(sum_up(y + 3, 1, 1))
    go(sum_down(y - 3, 0, 1))

    dha = ga * ua + gb * ub + gc * uc + gd * ud
    dhb = gb * ua - ga * ub - gc * ud + gd * uc
    dhc = gb * ud - ga * uc + gc * ua - gd * ub
    dhd = gc * ub - ga * ud - gb * uc + gd * ua
    dends[pl.ds(0, TRIP), :] = jnp.concatenate([dha, dhb, dhc, dhd], axis=1)
    gt[...] = select(hot_ends[...], dends[...], NN).reshape(N_REL, SLOTS, WIDTH)

    @pl.loop(16, N_REL)
    def _(k):
        exchange(gt, ret, b_s, b_r, k)

    @pl.loop(1, 16)
    def _(k):
        exchange(gt, ret, b_s, b_r, k)

    ret[rel] = gt[rel]

    for n in (1, 2, 3):
        for h in (1, 0):
            if n > 1 or h == 0:
                sum_up(y + 4 - n, h, n - 1).wait_recv()
                take(y + 4 - n, h, rp, n - 1)
                go(sum_up(y + 4 - n, h, n))
                sum_down(y - 4 + n, 1 - h, n - 1).wait_recv()
                take(y - 4 + n, 1 - h, rm, n - 1)
                go(sum_down(y - 4 + n, 1 - h, n))
    for h in (1, 0):
        sum_up(y, h, 3).wait_recv()
        sum_down(y, 1 - h, 3).wait_recv()
    ring[y] = ring[y] + (rp[3] + rm[3])

    far = {"dom": (1 - zh) * NY + y}
    cross = rcopy(ring.at[y, pl.ds(ZX, 8)], relx, rx_s, rx_r, far)
    go(cross)

    @pl.loop(1, ZX)
    def _(k):
        p = lax.rem(zi + k, ZX)
        rcopy(ring.at[y, p], zx_recv.at[zi], z_s.at[k], z_r.at[zi], zx_dev(p)).start()

    zx_recv[zi] = ring[y, zi]

    @pl.loop(1, ZX)
    def _(k):
        p = lax.rem(zi + k, ZX)
        rcopy(ring.at[y, p], zx_recv.at[p], z_s.at[k], z_r.at[p], zx_dev(p)).wait_recv()

    tile_out[...] = jnp.sum(zx_recv[...], axis=0)

    @pl.loop(1, N_DOM)
    def _(k):
        p = lax.rem(dom + k, N_DOM)
        rcopy(tile_out, t_recv.at[dom], t_s.at[k], t_r.at[dom], {"dom": p}).start()

    t_recv[dom] = tile_out[...]
    cross.wait_recv()
    rel_full[y] = ring[y, pl.ds(ZX, 8)] + relx[...]

    @pl.loop(1, NY)
    def _(k):
        to = {"dom": zh * NY + lax.rem(y + k, NY)}
        rcopy(rel_full.at[y], rel_full.at[y], ra_s.at[k], ra_r.at[y], to).start()

    @pl.loop(1, N_REL)
    def _(k):
        p = lax.rem(rel + k, N_REL)
        rcopy(gt.at[p], ret.at[p], b_s.at[k], b_r.at[p], {"rel": p}).wait_recv()

    send_hot = hot(ENT, slot_row(send_t))
    grad = select(send_hot, ret[...].reshape(N_REL * SLOTS, WIDTH), NN)

    @pl.loop(1, N_DOM)
    def _(k):
        p = lax.rem(dom + k, N_DOM)
        rcopy(tile_out, t_recv.at[p], t_s.at[k], t_r.at[p], {"dom": p}).wait_recv()

    total = jnp.concatenate(
        [
            jnp.concatenate([t_recv[g * 4 + w] for w in range(4)], axis=1)
            for g in range(4)
        ],
        axis=0,
    )
    owner = jnp.where(neg_part[...] == dom, 1.0, 0.0).astype(F32)
    neg_hot = hot(ENT, neg_rows[pl.ds(rel, 1), :])
    grad_e[...] = grad + owner * select(neg_hot, total, NN)

    @pl.loop(1, NY)
    def _(k):
        i = lax.rem(y + k, NY)
        there = rel_full.at[i]
        rcopy(there, there, ra_s.at[k], ra_r.at[i], {"dom": zh * NY + i}).wait_recv()

    for w in range(4):
        g = jnp.concatenate(
            [rel_full[yy, gg * 4 + w] for yy in range(NY) for gg in range(2)], axis=0
        )
        grad_r[:, pl.ds(w * 128, 128)] = g

    for c in sent:
        c.wait_send()

    @pl.loop(1, N_DOM)
    def _(k):
        p = lax.rem(dom + k, N_DOM)
        rcopy(neg_src.at[p], s1_recv.at[dom], s1_s.at[k], s1_r.at[dom], {"dom": p}).wait_send()
        rcopy(tile_out, t_recv.at[dom], t_s.at[k], t_r.at[dom], {"dom": p}).wait_send()

    @pl.loop(1, N_REL)
    def _(k):
        p = lax.rem(rel + k, N_REL)
        rcopy(send_buf.at[p], recv.at[rel], a_s.at[k], a_r.at[rel], {"rel": p}).wait_send()
        rcopy(gt.at[p], ret.at[rel], b_s.at[k], b_r.at[rel], {"rel": p}).wait_send()

    @pl.loop(1, ZX)
    def _(k):
        p = lax.rem(zi + k, ZX)
        here = nbuf.at[mine, zi]
        rcopy(here, here, s2_s.at[k], s2_r.at[zi], zx_dev(p)).wait_send()
        rcopy(ring.at[y, p], zx_recv.at[zi], z_s.at[k], z_r.at[zi], zx_dev(p)).wait_send()

    @pl.loop(1, NY)
    def _(k):
        to = {"dom": zh * NY + lax.rem(y + k, NY)}
        rcopy(rel_full.at[y], rel_full.at[y], ra_s.at[k], ra_r.at[y], to).wait_send()


def shards(
    entity, entity_acc, relation, relation_acc, send_rows, trip_head, trip_rel, trip_tail, neg_part, neg_rows,
):
    send_t = send_rows[0].T
    row = (1, TRIP)
    anywhere = pl.BlockSpec(memory_space=pl.ANY)
    vmem = pl.BlockSpec(memory_space=pltpu.VMEM)
    dma = pltpu.SemaphoreType.DMA
    rows = jax.ShapeDtypeStruct((ENT, WIDTH), F32)
    grad_e, grad_r = pl.pallas_call(
        kernel,
        out_shape=(rows, rows),
        in_specs=[anywhere] * 8,
        out_specs=(vmem, vmem),
        scratch_shapes=[
            pltpu.VMEM((ENT, WIDTH), F32),
            pltpu.VMEM((RELS, WIDTH), F32),
            pltpu.VMEM((SLOTS, N_REL), jnp.int32),
            pltpu.VMEM(row, jnp.int32),
            pltpu.VMEM(row, jnp.int32),
            pltpu.VMEM(row, jnp.int32),
            pltpu.VMEM((N_REL, NEG), jnp.int32),
            pltpu.VMEM((1, 1), jnp.int32),
            pltpu.VMEM((N_REL, SLOTS, WIDTH), F32),
            pltpu.VMEM((N_REL, SLOTS, WIDTH), F32),
            pltpu.VMEM((N_DOM, *TILE), F32),
            pltpu.VMEM((N_DOM, *TILE), F32),
            pltpu.VMEM((2 * NY, ZX, *TILE), F32),
            pltpu.VMEM((N_REL * SLOTS, 2 * TRIP), BF16),
            pltpu.VMEM((2 * TRIP, WIDTH), F32),
            pltpu.VMEM((TRIP, WIDTH), F32),
            pltpu.VMEM((TRIP, WIDTH), F32),
            pltpu.VMEM((TRIP, WIDTH), F32),
            pltpu.VMEM((2 * TRIP, WIDTH), F32),
            pltpu.VMEM((2 * NY, ZX, *TILE), F32),
            pltpu.VMEM((NY, ZX, *TILE), F32),
            pltpu.VMEM((NY, ZX + 8, *TILE), F32),
            pltpu.VMEM((4, ZX + 8, *TILE), F32),
            pltpu.VMEM((4, ZX + 8, *TILE), F32),
            pltpu.VMEM((ZX, *TILE), F32),
            pltpu.VMEM((8, *TILE), F32),
            pltpu.VMEM(TILE, F32),
            pltpu.VMEM((N_DOM, *TILE), F32),
            pltpu.VMEM((NY, 8, *TILE), F32),
            pltpu.VMEM((N_REL, SLOTS, WIDTH), F32),
            pltpu.VMEM((N_REL, SLOTS, WIDTH), F32),
            dma((8,)), dma((N_REL,)), dma((N_REL,)), dma((N_REL,)), dma((N_REL,)),
            dma((N_DOM,)), dma((N_DOM,)), dma((ZX,)), dma((ZX,)),
            dma((8,)), dma((8,)), dma((8,)), dma((8,)),
            dma((16,)), dma((16,)), dma, dma,
            dma((8,)), dma((8,)), dma((8,)), dma((8,)),
            dma((ZX,)), dma((ZX,)), dma, dma,
            dma((N_DOM,)), dma((N_DOM,)), dma((NY,)), dma((NY,)),
        ],
        compiler_params=pltpu.CompilerParams(
            collective_id=0, has_side_effects=True, vmem_limit_bytes=56 << 20
        ),
        name="step",
    )(
        entity, relation, send_t, trip_head.reshape(row), trip_tail.reshape(row),
        trip_rel.reshape(row), neg_rows, neg_part.reshape(1, 1),
    )
    return (
        *adagrad(entity, entity_acc, grad_e),
        *adagrad(relation, relation_acc, grad_r),
    )


def solution(mesh):
    both = ("dom", "rel")
    in_specs = (
        P(both, None), P(both, None), P("rel", None), P("rel", None), P(both, None, None),
        P(both), P(both), P(both), P(), P(),
    )
    out_specs = (P(both, None), P(both, None), P("rel", None), P("rel", None))
    return jax.shard_map(shards, mesh=mesh, in_specs=in_specs, out_specs=out_specs, check_vma=False)
```

```python
import jax
import jax.numpy as jnp
from jax import lax
from jax.experimental import pallas as pl
from jax.experimental.pallas import tpu as pltpu
from jax.sharding import PartitionSpec as P

MESH = pl.DeviceIdType.MESH
F32, BF16 = jnp.float32, jnp.bfloat16
step_size = 0.05

N_DOM, N_REL = 16, 32
NY, NX = 8, 4
ZX = 32
ENT, RELS, TRIP, SLOTS, NEG, WIDTH = 128, 128, 256, 16, 32, 512
TILE = (8, 128)
NEGS = NEG * N_REL
AHEAD = (8, 12, 15, 18, 21, 24, 27, 32)
BACK = (9, 12, 14, 16, 18, 20, 32)
HALF = ZX // 2
CUT = 20

NN = (((1,), (0,)), ((), ()))
TN = (((0,), (0,)), ((), ()))
NT = (((1,), (1,)), ((), ()))


def mm(a, b, dims):
    return lax.dot_general(a, b, dims, preferred_element_type=F32)


def halves(v):
    hi = v.astype(BF16)
    return hi, (v - hi.astype(F32)).astype(BF16)


def select(one_hot, v, dims):
    hi, lo = halves(v)
    return mm(one_hot, hi, dims) + mm(one_hot, lo, dims)


def mm3(a, b, dims):
    return mm(a[0], b[0], dims) + (mm(a[0], b[1], dims) + mm(a[1], b[0], dims))


def hot(rows, index_row):
    n = index_row.shape[1]
    at = lax.broadcasted_iota(jnp.int32, (rows, n), 0)
    return jnp.where(at == index_row, 1.0, 0.0).astype(BF16)


def slot_row(send_t):
    n = N_REL * SLOTS
    at = lax.broadcasted_iota(jnp.int32, (N_REL, n), 1)
    spread = lax.div(at, SLOTS) == lax.broadcasted_iota(jnp.int32, (N_REL, n), 0)
    full = mm(
        send_t[...].astype(F32).astype(BF16), jnp.where(spread, 1.0, 0.0).astype(BF16), NN
    )
    slot = lax.rem(lax.broadcasted_iota(jnp.int32, (SLOTS, n), 1), SLOTS)
    keep = slot == lax.broadcasted_iota(jnp.int32, (SLOTS, n), 0)
    return jnp.sum(jnp.where(keep, full, 0.0), axis=0, keepdims=True).astype(jnp.int32)


def rcopy(src, dst, ssem, rsem, dev):
    return pltpu.make_async_remote_copy(
        src_ref=src, dst_ref=dst, send_sem=ssem, recv_sem=rsem, device_id=dev, device_id_type=MESH
    )


def quarter(v):
    return v[:, 0:128], v[:, 128:256], v[:, 256:384], v[:, 384:512]


def adagrad(values, history, gradient):
    history_new = history + gradient * gradient
    return values - step_size * gradient / jnp.sqrt(history_new), history_new


def kernel(
    entity_h, relation_h, send_h, head_h, tail_h, rels_h, neg_h, part_h,
    grad_e, grad_r,
    entity, relation, send_t, head_row, tail_row, rels_row, neg_rows, neg_part,
    send_buf, recv, neg_src, s1_recv, nbuf, hot_ends, ends, rot, query, dq, dends,
    gall, xrecv, ring, rp, rm, zx_recv, relx, tile_out, t_recv, rel_full, gt, ret,
    in_s, a_s, a_r, b_s, b_r, s1_s, s1_r, s2_s, s2_r, yp_s, yp_r, ym_s, ym_r, sib_s, sib_r, x_s, x_r,
    rp_s, rp_r, rm_s, rm_r, z_s, z_r, rx_s, rx_r, t_s, t_r, ra_s, ra_r,
):
    loads = [
        pltpu.make_async_copy(h, v, in_s.at[n])
        for n, (h, v) in enumerate(
            (
                (entity_h, entity), (neg_h, neg_rows), (send_h, send_t), (part_h, neg_part),
                (head_h, head_row), (tail_h, tail_row), (rels_h, rels_row), (relation_h, relation),
            )
        )
    ]
    for c in loads:
        c.start()
    dom, rel = lax.axis_index("dom"), lax.axis_index("rel")
    zh, y = lax.div(dom, NY), lax.rem(dom, NY)
    zx_low, core = lax.div(rel, 2), lax.rem(rel, 2)
    zi = zh * 16 + zx_low
    up, down = lax.rem(y + 1, NY), lax.rem(y + NY - 1, NY)
    up_dev, down_dev = {"dom": zh * NY + up}, {"dom": zh * NY + down}
    sib_dev = {"rel": zx_low * 2 + (1 - core)}

    def zx_dev(p):
        return {"dom": lax.div(p, 16) * NY + y, "rel": lax.rem(p, 16) * 2 + core}

    barrier = pltpu.get_barrier_semaphore()

    @pl.loop(1, N_DOM)
    def _(k):
        pl.semaphore_signal(
            barrier, inc=1, device_id={"dom": lax.rem(dom + k, N_DOM)}, device_id_type=MESH
        )

    @pl.loop(1, N_REL)
    def _(k):
        pl.semaphore_signal(
            barrier, inc=1, device_id={"rel": lax.rem(rel + k, N_REL)}, device_id_type=MESH
        )

    @pl.loop(1, 16)
    def _(k):
        p = (1 - zh) * 16 + lax.rem(zx_low + k, 16)
        pl.semaphore_signal(barrier, inc=1, device_id=zx_dev(p), device_id_type=MESH)

    for c in loads[:4]:
        c.wait()
    ent = halves(entity[...])
    neg_hot = hot(ENT, neg_rows[pl.ds(rel, 1), :])
    own = mm(neg_hot, ent[0], TN) + mm(neg_hot, ent[1], TN)
    for g in range(4):
        for w in range(4):
            neg_src[g * 4 + w] = own[g * 8 : g * 8 + 8, w * 128 : w * 128 + 128]
    send_hot = hot(ENT, slot_row(send_t))
    rows = mm(send_hot, ent[0], TN) + mm(send_hot, ent[1], TN)
    send_buf[...] = rows.reshape(N_REL, SLOTS, WIDTH)
    for c in loads[4:]:
        c.wait()
    is_root = lax.broadcasted_iota(jnp.int32, (N_DOM, 1, 1), 0) == neg_part[...].reshape(1, 1, 1)

    pl.semaphore_wait(barrier, (N_DOM - 1) + (N_REL - 1) + 15)

    @pl.loop(1, N_DOM)
    def _(k):
        p = lax.rem(dom + k, N_DOM)
        rcopy(neg_src.at[p], s1_recv.at[dom], s1_s.at[k], s1_r.at[dom], {"dom": p}).start()

    def peer(k):
        pz = lax.rem(lax.div(rel, 8) + lax.rem(k, 4), 4)
        px = lax.rem(lax.div(lax.rem(rel, 8), 2) + lax.div(k, 8), NX)
        pc = lax.rem(core + lax.rem(lax.div(k, 4), 2), 2)
        return pz * 8 + px * 2 + pc

    def exchange(src, dst, ssem, rsem, lo, hi):
        @pl.loop(lo, hi)
        def _(k):
            p = peer(k)
            rcopy(src.at[p], dst.at[rel], ssem.at[k], rsem.at[rel], {"rel": p}).start()

    def ahead(n):
        exchange(send_buf, recv, a_s, a_r, AHEAD[n - 1] if n else 1, AHEAD[n])

    def back(n):
        exchange(gt, ret, b_s, b_r, BACK[n - 1] if n else 1, BACK[n])

    ahead(0)

    s1_recv[dom] = neg_src[dom]
    recv[rel] = send_buf[rel]

    @pl.loop(1, N_DOM)
    def _(k):
        p = lax.rem(dom + k, N_DOM)
        rcopy(neg_src.at[p], s1_recv.at[p], s1_s.at[k], s1_r.at[p], {"dom": p}).wait_recv()

    mine = core * NY + y
    nbuf[mine, zi] = jnp.sum(jnp.where(is_root, s1_recv[...], 0.0), axis=0)

    @pl.loop(1, ZX)
    def _(k):
        p = lax.rem(zi + k, ZX)
        here = nbuf.at[mine, zi]
        rcopy(here, here, s2_s.at[k], s2_r.at[zi], zx_dev(p)).start()

    ahead(1)

    @pl.loop(1, ZX)
    def _(k):
        p = lax.rem(zi + k, ZX)
        there = nbuf.at[mine, p]
        rcopy(there, there, s2_s.at[k], s2_r.at[p], zx_dev(p)).wait_recv()

    def part(core_of, yy, h):
        return nbuf.at[core_of * NY + lax.rem(yy + 2 * NY, NY), pl.ds(h * HALF, HALF)]

    def pass_up(yy, h, n):
        ref = part(core, yy, h)
        return rcopy(ref, ref, yp_s.at[2 * n + h], yp_r.at[2 * n + h], up_dev)

    def pass_down(yy, h, n):
        ref = part(core, yy, h)
        return rcopy(ref, ref, ym_s.at[2 * n + h], ym_r.at[2 * n + h], down_dev)

    def to_sib(core_of, off, h):
        ref = part(core_of, y + off, h)
        at = 2 * (off + 4) + h
        return rcopy(ref, ref, sib_s.at[at], sib_r.at[at], sib_dev)

    sent = []

    def go(c):
        c.start()
        sent.append(c)

    for h in (0, 1):
        go(pass_up(y, h, 0))
        go(pass_down(y, h, 0))
    for h in (0, 1):
        go(to_sib(core, 0, h))
    for n in (1, 2, 3):
        for h in (0, 1):
            pass_up(y - n, h, n - 1).wait_recv()
            if n < 3 or h == 0:
                go(pass_up(y - n, h, n))
            go(to_sib(core, -n, h))
            pass_down(y + n, h, n - 1).wait_recv()
            if n < 3 or h == 1:
                go(pass_down(y + n, h, n))
            go(to_sib(core, n, h))
            ahead(2 * n + h)

    @pl.loop(1, N_REL)
    def _(k):
        p = lax.rem(rel + k, N_REL)
        rcopy(send_buf.at[p], recv.at[p], a_s.at[k], a_r.at[p], {"rel": p}).wait_recv()

    hot_ends[:, pl.ds(0, TRIP)] = hot(N_REL * SLOTS, head_row[...])
    hot_ends[:, pl.ds(TRIP, TRIP)] = hot(N_REL * SLOTS, tail_row[...])
    ends[...] = select(hot_ends[...], recv[...].reshape(N_REL * SLOTS, WIDTH), TN)
    rel_hot = hot(RELS, rels_row[...])
    ra, rb, rc, rd = quarter(relation[...])
    inv = 1.0 / jnp.sqrt(ra * ra + rb * rb + rc * rc + rd * rd)
    unit = jnp.concatenate([ra * inv, rb * inv, rc * inv, rd * inv], axis=1)
    rot[...] = select(rel_hot, unit, TN)
    ha, hb, hc, hd = quarter(ends[pl.ds(0, TRIP), :])
    ua, ub, uc, ud = quarter(rot[...])
    qa = ha * ua - hb * ub - hc * uc - hd * ud
    qb = ha * ub + hb * ua + hc * ud - hd * uc
    qc = ha * uc - hb * ud + hc * ua + hd * ub
    qd = ha * ud + hb * uc - hc * ub + hd * ua
    query[...] = jnp.concatenate([qa, qb, qc, qd], axis=1)
    tails = ends[pl.ds(TRIP, TRIP), :]
    positive = jnp.sum(query[...] * tails, axis=1, keepdims=True)
    pull = -1.0 / (1.0 + jnp.exp(positive))
    dq[...] = pull * tails
    dends[pl.ds(TRIP, TRIP), :] = pull * query[...]

    pass_up(y - 4, 0, 3).wait_recv()
    go(to_sib(core, -4, 0))
    pass_down(y + 4, 1, 3).wait_recv()
    go(to_sib(core, -4, 1))
    for off in (0, -1, 1, -2, 2, -3, 3, -4):
        for h in (0, 1):
            to_sib(1 - core, off, h).wait_recv()

    def score(b):
        q = halves(query[...])
        n = halves(
            jnp.concatenate(
                [nbuf[b * 4 + w].reshape(ZX * 8, 128) for w in range(4)], axis=1
            )
        )
        s = mm3(q, n, NT)
        p = halves((1.0 / NEGS) / (1.0 + jnp.exp(-s)))
        dq[...] += mm3(p, n, NN)
        dn = mm3(p, q, TN)
        for w in range(4):
            gall[b * 4 + w] = dn[:, w * 128 : w * 128 + 128].reshape(ZX, 8, 128)

    swap = rcopy(gall.at[pl.ds((1 - core) * NY, NY)], xrecv, x_s, x_r, sib_dev)

    @pl.loop(0, 2)
    def _(b):
        score((1 - core) * 2 + b)

    go(swap)

    @pl.loop(0, 2)
    def _(b):
        score(core * 2 + b)

    ga, gb, gc, gd = quarter(dq[...])
    ha, hb, hc, hd = quarter(ends[pl.ds(0, TRIP), :])
    ua, ub, uc, ud = quarter(rot[...])
    dua = ga * ha + gb * hb + gc * hc + gd * hd
    dub = gb * ha - ga * hb + gc * hd - gd * hc
    duc = gc * ha - ga * hc - gb * hd + gd * hb
    dud = gb * hc - ga * hd - gc * hb + gd * ha
    rel_hot = hot(RELS, rels_row[...])
    du = select(rel_hot, jnp.concatenate([dua, dub, duc, dud], axis=1), NN)
    ra, rb, rc, rd = quarter(relation[...])
    inv = 1.0 / jnp.sqrt(ra * ra + rb * rb + rc * rc + rd * rd)
    va, vb, vc, vd = ra * inv, rb * inv, rc * inv, rd * inv
    da, db, dc, dd = quarter(du)
    along = da * va + db * vb + dc * vc + dd * vd
    parts = [(g - v * along) * inv for g, v in ((da, va), (db, vb), (dc, vc), (dd, vd))]
    for yy in range(NY):
        for g in range(2):
            for w in range(4):
                at = yy * 16 + g * 8
                ring[yy, ZX + g * 4 + w] = parts[w][at : at + 8, :]

    rcopy(gall.at[pl.ds(core * NY, NY)], xrecv, x_s, x_r, sib_dev).wait_recv()

    @pl.loop(0, NY)
    def _(k):
        ring[k, pl.ds(0, ZX)] = gall[core * NY + k] + xrecv[k]

    def chunk(yy, h):
        return ring.at[lax.rem(yy + 2 * NY, NY), pl.ds(h * CUT, CUT)]

    def take(yy, h, got, n):
        i = lax.rem(yy + 2 * NY, NY)
        cols = pl.ds(h * CUT, CUT)
        ring[i, cols] = ring[i, cols] + got[n, cols]

    def sum_up(yy, h, n):
        at = 2 * n + h
        dst = rp.at[n, pl.ds(h * CUT, CUT)]
        return rcopy(chunk(yy, h), dst, rp_s.at[at], rp_r.at[at], up_dev)

    def sum_down(yy, h, n):
        at = 2 * n + h
        dst = rm.at[n, pl.ds(h * CUT, CUT)]
        return rcopy(chunk(yy, h), dst, rm_s.at[at], rm_r.at[at], down_dev)

    go(sum_up(y + 4, 0, 0))
    go(sum_down(y - 4, 1, 0))
    go(sum_up(y + 3, 1, 1))
    go(sum_down(y - 3, 0, 1))

    dha = ga * ua + gb * ub + gc * uc + gd * ud
    dhb = gb * ua - ga * ub - gc * ud + gd * uc
    dhc = gb * ud - ga * uc + gc * ua - gd * ub
    dhd = gc * ub - ga * ud - gb * uc + gd * ua
    dends[pl.ds(0, TRIP), :] = jnp.concatenate([dha, dhb, dhc, dhd], axis=1)
    gt[...] = select(hot_ends[...], dends[...], NN).reshape(N_REL, SLOTS, WIDTH)

    ret[rel] = gt[rel]
    back(0)

    for n in (1, 2, 3):
        for h in (1, 0):
            if n > 1 or h == 0:
                sum_up(y + 4 - n, h, n - 1).wait_recv()
                take(y + 4 - n, h, rp, n - 1)
                go(sum_up(y + 4 - n, h, n))
                sum_down(y - 4 + n, 1 - h, n - 1).wait_recv()
                take(y - 4 + n, 1 - h, rm, n - 1)
                go(sum_down(y - 4 + n, 1 - h, n))
                back(2 * n - 1 - h)
    for h in (1, 0):
        sum_up(y, h, 3).wait_recv()
        sum_down(y, 1 - h, 3).wait_recv()
    ring[y] = ring[y] + (rp[3] + rm[3])

    far = {"dom": (1 - zh) * NY + y}
    cross = rcopy(ring.at[y, pl.ds(ZX, 8)], relx, rx_s, rx_r, far)
    go(cross)

    @pl.loop(1, ZX)
    def _(k):
        p = lax.rem(zi + k, ZX)
        rcopy(ring.at[y, p], zx_recv.at[zi], z_s.at[k], z_r.at[zi], zx_dev(p)).start()

    back(6)
    zx_recv[zi] = ring[y, zi]

    @pl.loop(1, ZX)
    def _(k):
        p = lax.rem(zi + k, ZX)
        rcopy(ring.at[y, p], zx_recv.at[p], z_s.at[k], z_r.at[p], zx_dev(p)).wait_recv()

    tile_out[...] = jnp.sum(zx_recv[...], axis=0)

    @pl.loop(1, N_DOM)
    def _(k):
        p = lax.rem(dom + k, N_DOM)
        rcopy(tile_out, t_recv.at[dom], t_s.at[k], t_r.at[dom], {"dom": p}).start()

    t_recv[dom] = tile_out[...]
    cross.wait_recv()
    rel_full[y] = ring[y, pl.ds(ZX, 8)] + relx[...]

    @pl.loop(1, NY)
    def _(k):
        to = {"dom": zh * NY + lax.rem(y + k, NY)}
        rcopy(rel_full.at[y], rel_full.at[y], ra_s.at[k], ra_r.at[y], to).start()

    @pl.loop(1, N_REL)
    def _(k):
        p = lax.rem(rel + k, N_REL)
        rcopy(gt.at[p], ret.at[p], b_s.at[k], b_r.at[p], {"rel": p}).wait_recv()

    send_hot = hot(ENT, slot_row(send_t))
    grad = select(send_hot, ret[...].reshape(N_REL * SLOTS, WIDTH), NN)

    @pl.loop(1, N_DOM)
    def _(k):
        p = lax.rem(dom + k, N_DOM)
        rcopy(tile_out, t_recv.at[p], t_s.at[k], t_r.at[p], {"dom": p}).wait_recv()

    total = jnp.concatenate(
        [
            jnp.concatenate([t_recv[g * 4 + w] for w in range(4)], axis=1)
            for g in range(4)
        ],
        axis=0,
    )
    owner = jnp.where(neg_part[...] == dom, 1.0, 0.0).astype(F32)
    neg_hot = hot(ENT, neg_rows[pl.ds(rel, 1), :])
    grad_e[...] = grad + owner * select(neg_hot, total, NN)

    @pl.loop(1, NY)
    def _(k):
        i = lax.rem(y + k, NY)
        there = rel_full.at[i]
        rcopy(there, there, ra_s.at[k], ra_r.at[i], {"dom": zh * NY + i}).wait_recv()

    for w in range(4):
        g = jnp.concatenate(
            [rel_full[yy, gg * 4 + w] for yy in range(NY) for gg in range(2)], axis=0
        )
        grad_r[:, pl.ds(w * 128, 128)] = g

    for c in sent:
        c.wait_send()

    @pl.loop(1, N_DOM)
    def _(k):
        p = lax.rem(dom + k, N_DOM)
        rcopy(neg_src.at[p], s1_recv.at[dom], s1_s.at[k], s1_r.at[dom], {"dom": p}).wait_send()
        rcopy(tile_out, t_recv.at[dom], t_s.at[k], t_r.at[dom], {"dom": p}).wait_send()

    @pl.loop(1, N_REL)
    def _(k):
        p = lax.rem(rel + k, N_REL)
        rcopy(send_buf.at[p], recv.at[rel], a_s.at[k], a_r.at[rel], {"rel": p}).wait_send()
        rcopy(gt.at[p], ret.at[rel], b_s.at[k], b_r.at[rel], {"rel": p}).wait_send()

    @pl.loop(1, ZX)
    def _(k):
        p = lax.rem(zi + k, ZX)
        here = nbuf.at[mine, zi]
        rcopy(here, here, s2_s.at[k], s2_r.at[zi], zx_dev(p)).wait_send()
        rcopy(ring.at[y, p], zx_recv.at[zi], z_s.at[k], z_r.at[zi], zx_dev(p)).wait_send()

    @pl.loop(1, NY)
    def _(k):
        to = {"dom": zh * NY + lax.rem(y + k, NY)}
        rcopy(rel_full.at[y], rel_full.at[y], ra_s.at[k], ra_r.at[y], to).wait_send()


def shards(
    entity, entity_acc, relation, relation_acc, send_rows, trip_head, trip_rel, trip_tail, neg_part, neg_rows,
):
    send_t = send_rows[0].T
    row = (1, TRIP)
    anywhere = pl.BlockSpec(memory_space=pl.ANY)
    vmem = pl.BlockSpec(memory_space=pltpu.VMEM)
    dma = pltpu.SemaphoreType.DMA
    rows = jax.ShapeDtypeStruct((ENT, WIDTH), F32)
    grad_e, grad_r = pl.pallas_call(
        kernel,
        out_shape=(rows, rows),
        in_specs=[anywhere] * 8,
        out_specs=(vmem, vmem),
        scratch_shapes=[
            pltpu.VMEM((ENT, WIDTH), F32),
            pltpu.VMEM((RELS, WIDTH), F32),
            pltpu.VMEM((SLOTS, N_REL), jnp.int32),
            pltpu.VMEM(row, jnp.int32),
            pltpu.VMEM(row, jnp.int32),
            pltpu.VMEM(row, jnp.int32),
            pltpu.VMEM((N_REL, NEG), jnp.int32),
            pltpu.VMEM((1, 1), jnp.int32),
            pltpu.VMEM((N_REL, SLOTS, WIDTH), F32),
            pltpu.VMEM((N_REL, SLOTS, WIDTH), F32),
            pltpu.VMEM((N_DOM, *TILE), F32),
            pltpu.VMEM((N_DOM, *TILE), F32),
            pltpu.VMEM((2 * NY, ZX, *TILE), F32),
            pltpu.VMEM((N_REL * SLOTS, 2 * TRIP), BF16),
            pltpu.VMEM((2 * TRIP, WIDTH), F32),
            pltpu.VMEM((TRIP, WIDTH), F32),
            pltpu.VMEM((TRIP, WIDTH), F32),
            pltpu.VMEM((TRIP, WIDTH), F32),
            pltpu.VMEM((2 * TRIP, WIDTH), F32),
            pltpu.VMEM((2 * NY, ZX, *TILE), F32),
            pltpu.VMEM((NY, ZX, *TILE), F32),
            pltpu.VMEM((NY, ZX + 8, *TILE), F32),
            pltpu.VMEM((4, ZX + 8, *TILE), F32),
            pltpu.VMEM((4, ZX + 8, *TILE), F32),
            pltpu.VMEM((ZX, *TILE), F32),
            pltpu.VMEM((8, *TILE), F32),
            pltpu.VMEM(TILE, F32),
            pltpu.VMEM((N_DOM, *TILE), F32),
            pltpu.VMEM((NY, 8, *TILE), F32),
            pltpu.VMEM((N_REL, SLOTS, WIDTH), F32),
            pltpu.VMEM((N_REL, SLOTS, WIDTH), F32),
            dma((8,)), dma((N_REL,)), dma((N_REL,)), dma((N_REL,)), dma((N_REL,)),
            dma((N_DOM,)), dma((N_DOM,)), dma((ZX,)), dma((ZX,)),
            dma((8,)), dma((8,)), dma((8,)), dma((8,)),
            dma((16,)), dma((16,)), dma, dma,
            dma((8,)), dma((8,)), dma((8,)), dma((8,)),
            dma((ZX,)), dma((ZX,)), dma, dma,
            dma((N_DOM,)), dma((N_DOM,)), dma((NY,)), dma((NY,)),
        ],
        compiler_params=pltpu.CompilerParams(
            collective_id=0, has_side_effects=True, vmem_limit_bytes=56 << 20
        ),
        name="step",
    )(
        entity, relation, send_t, trip_head.reshape(row), trip_tail.reshape(row),
        trip_rel.reshape(row), neg_rows, neg_part.reshape(1, 1),
    )
    return (
        *adagrad(entity, entity_acc, grad_e),
        *adagrad(relation, relation_acc, grad_r),
    )


def solution(mesh):
    both = ("dom", "rel")
    in_specs = (
        P(both, None), P(both, None), P("rel", None), P("rel", None), P(both, None, None),
        P(both), P(both), P(both), P(), P(),
    )
    out_specs = (P(both, None), P(both, None), P("rel", None), P("rel", None))
    return jax.shard_map(shards, mesh=mesh, in_specs=in_specs, out_specs=out_specs, check_vma=False)
```

```python
import jax
import jax.numpy as jnp
from jax import lax
from jax.experimental import pallas as pl
from jax.experimental.pallas import tpu as pltpu
from jax.sharding import PartitionSpec as P

MESH = pl.DeviceIdType.MESH
F32, BF16 = jnp.float32, jnp.bfloat16
step_size = 0.05

N_DOM, N_REL = 16, 32
NY, NX = 8, 4
ZX = 32
ENT, RELS, TRIP, SLOTS, NEG, WIDTH = 128, 128, 256, 16, 32, 512
TILE = (8, 128)
NEGS = NEG * N_REL
AHEAD = (11, 18, 20, 22, 24, 26, 28, 32)
BACK = (9, 12, 14, 16, 18, 20, 32)
HALF = ZX // 2
CUT = 20

NN = (((1,), (0,)), ((), ()))
TN = (((0,), (0,)), ((), ()))
NT = (((1,), (1,)), ((), ()))


def mm(a, b, dims):
    return lax.dot_general(a, b, dims, preferred_element_type=F32)


def halves(v):
    hi = v.astype(BF16)
    return hi, (v - hi.astype(F32)).astype(BF16)


def select(one_hot, v, dims):
    hi, lo = halves(v)
    return mm(one_hot, hi, dims) + mm(one_hot, lo, dims)


def mm3(a, b, dims):
    return mm(a[0], b[0], dims) + (mm(a[0], b[1], dims) + mm(a[1], b[0], dims))


def hot(rows, index_row):
    n = index_row.shape[1]
    at = lax.broadcasted_iota(jnp.int32, (rows, n), 0)
    return jnp.where(at == index_row, 1.0, 0.0).astype(BF16)


def slot_row(send_t):
    n = N_REL * SLOTS
    at = lax.broadcasted_iota(jnp.int32, (N_REL, n), 1)
    spread = lax.div(at, SLOTS) == lax.broadcasted_iota(jnp.int32, (N_REL, n), 0)
    full = mm(
        send_t[...].astype(F32).astype(BF16), jnp.where(spread, 1.0, 0.0).astype(BF16), NN
    )
    slot = lax.rem(lax.broadcasted_iota(jnp.int32, (SLOTS, n), 1), SLOTS)
    keep = slot == lax.broadcasted_iota(jnp.int32, (SLOTS, n), 0)
    return jnp.sum(jnp.where(keep, full, 0.0), axis=0, keepdims=True).astype(jnp.int32)


def rcopy(src, dst, ssem, rsem, dev):
    return pltpu.make_async_remote_copy(
        src_ref=src, dst_ref=dst, send_sem=ssem, recv_sem=rsem, device_id=dev, device_id_type=MESH
    )


def quarter(v):
    return v[:, 0:128], v[:, 128:256], v[:, 256:384], v[:, 384:512]


def adagrad(values, history, gradient):
    history_new = history + gradient * gradient
    return values - step_size * gradient / jnp.sqrt(history_new), history_new


def kernel(
    entity_h, relation_h, send_h, head_h, tail_h, rels_h, neg_h, part_h,
    grad_e, grad_r,
    entity, relation, send_t, head_row, tail_row, rels_row, neg_rows, neg_part,
    send_buf, recv, neg_src, s1_recv, nbuf, hot_ends, ends, rot, query, dq, dends,
    rel_hot, unit, scale, q_hi, q_lo,
    gall, xrecv, ring, rp, rm, zx_recv, relx, tile_out, t_recv, rel_full, gt, ret,
    in_s, a_s, a_r, b_s, b_r, s1_s, s1_r, s2_s, s2_r, yp_s, yp_r, ym_s, ym_r, sib_s, sib_r, x_s, x_r,
    rp_s, rp_r, rm_s, rm_r, z_s, z_r, rx_s, rx_r, t_s, t_r, ra_s, ra_r,
):
    loads = [
        pltpu.make_async_copy(h, v, in_s.at[n])
        for n, (h, v) in enumerate(
            (
                (entity_h, entity), (neg_h, neg_rows), (send_h, send_t), (part_h, neg_part),
                (head_h, head_row), (tail_h, tail_row), (rels_h, rels_row), (relation_h, relation),
            )
        )
    ]
    for c in loads:
        c.start()
    dom, rel = lax.axis_index("dom"), lax.axis_index("rel")
    zh, y = lax.div(dom, NY), lax.rem(dom, NY)
    zx_low, core = lax.div(rel, 2), lax.rem(rel, 2)
    zi = zh * 16 + zx_low
    up, down = lax.rem(y + 1, NY), lax.rem(y + NY - 1, NY)
    up_dev, down_dev = {"dom": zh * NY + up}, {"dom": zh * NY + down}
    sib_dev = {"rel": zx_low * 2 + (1 - core)}

    def zx_dev(p):
        return {"dom": lax.div(p, 16) * NY + y, "rel": lax.rem(p, 16) * 2 + core}

    def fan(j, n):
        return n // 2 + lax.div(j + 1, 2) * (1 - 2 * lax.rem(j, 2))

    def zx_peer(j):
        return lax.rem(zi + fan(j, ZX), ZX)

    def dom_peer(j):
        other = lax.rem(zh + 1 - lax.div(j, NY), 2)
        return other * NY + lax.rem(y + fan(lax.rem(j, NY), NY), NY)

    barrier = pltpu.get_barrier_semaphore()

    @pl.loop(0, N_DOM - 1)
    def _(k):
        pl.semaphore_signal(
            barrier, inc=1, device_id={"dom": dom_peer(k)}, device_id_type=MESH
        )

    @pl.loop(1, N_REL)
    def _(k):
        pl.semaphore_signal(
            barrier, inc=1, device_id={"rel": lax.rem(rel + k, N_REL)}, device_id_type=MESH
        )

    @pl.loop(1, 16)
    def _(k):
        p = (1 - zh) * 16 + lax.rem(zx_low + k, 16)
        pl.semaphore_signal(barrier, inc=1, device_id=zx_dev(p), device_id_type=MESH)

    for c in loads[:4]:
        c.wait()
    ent = halves(entity[...])
    neg_hot = hot(ENT, neg_rows[pl.ds(rel, 1), :])
    own = mm(neg_hot, ent[0], TN) + mm(neg_hot, ent[1], TN)
    for g in range(4):
        for w in range(4):
            neg_src[g * 4 + w] = own[g * 8 : g * 8 + 8, w * 128 : w * 128 + 128]
    send_hot = hot(ENT, slot_row(send_t))
    rows = mm(send_hot, ent[0], TN) + mm(send_hot, ent[1], TN)
    send_buf[...] = rows.reshape(N_REL, SLOTS, WIDTH)
    for c in loads[4:]:
        c.wait()
    is_root = lax.broadcasted_iota(jnp.int32, (N_DOM, 1, 1), 0) == neg_part[...].reshape(1, 1, 1)

    pl.semaphore_wait(barrier, (N_DOM - 1) + (N_REL - 1) + 15)

    @pl.loop(0, N_DOM - 1)
    def _(k):
        p = dom_peer(k)
        rcopy(neg_src.at[p], s1_recv.at[dom], s1_s.at[k], s1_r.at[dom], {"dom": p}).start()

    def peer(k):
        pz = lax.rem(lax.div(rel, 8) + lax.rem(k, 4), 4)
        px = lax.rem(lax.div(lax.rem(rel, 8), 2) + lax.div(k, 8), NX)
        pc = lax.rem(core + lax.rem(lax.div(k, 4), 2), 2)
        return pz * 8 + px * 2 + pc

    def exchange(src, dst, ssem, rsem, lo, hi):
        @pl.loop(lo, hi)
        def _(k):
            p = peer(k)
            rcopy(src.at[p], dst.at[rel], ssem.at[k], rsem.at[rel], {"rel": p}).start()

    def ahead(n):
        exchange(send_buf, recv, a_s, a_r, AHEAD[n - 1] if n else 1, AHEAD[n])

    def back(n):
        exchange(gt, ret, b_s, b_r, BACK[n - 1] if n else 1, BACK[n])

    ahead(0)

    s1_recv[dom] = neg_src[dom]
    recv[rel] = send_buf[rel]

    @pl.loop(0, N_DOM - 1)
    def _(k):
        p = dom_peer(k)
        rcopy(neg_src.at[p], s1_recv.at[p], s1_s.at[k], s1_r.at[p], {"dom": p}).wait_recv()

    mine = core * NY + y
    nbuf[mine, zi] = jnp.sum(jnp.where(is_root, s1_recv[...], 0.0), axis=0)

    @pl.loop(0, ZX - 1)
    def _(k):
        p = zx_peer(k)
        here = nbuf.at[mine, zi]
        rcopy(here, here, s2_s.at[k], s2_r.at[zi], zx_dev(p)).start()

    ahead(1)

    @pl.loop(0, ZX - 1)
    def _(k):
        p = zx_peer(k)
        there = nbuf.at[mine, p]
        rcopy(there, there, s2_s.at[k], s2_r.at[p], zx_dev(p)).wait_recv()

    def part(core_of, yy, h):
        return nbuf.at[core_of * NY + lax.rem(yy + 2 * NY, NY), pl.ds(h * HALF, HALF)]

    def pass_up(yy, h, n):
        ref = part(core, yy, h)
        return rcopy(ref, ref, yp_s.at[2 * n + h], yp_r.at[2 * n + h], up_dev)

    def pass_down(yy, h, n):
        ref = part(core, yy, h)
        return rcopy(ref, ref, ym_s.at[2 * n + h], ym_r.at[2 * n + h], down_dev)

    def to_sib(core_of, off, h):
        ref = part(core_of, y + off, h)
        at = 2 * (off + 4) + h
        return rcopy(ref, ref, sib_s.at[at], sib_r.at[at], sib_dev)

    sent = []

    def go(c):
        c.start()
        sent.append(c)

    for h in (0, 1):
        go(pass_up(y, h, 0))
        go(pass_down(y, h, 0))
    for h in (0, 1):
        go(to_sib(core, 0, h))
    for n in (1, 2, 3):
        for h in (0, 1):
            pass_up(y - n, h, n - 1).wait_recv()
            if n < 3 or h == 0:
                go(pass_up(y - n, h, n))
            go(to_sib(core, -n, h))
            pass_down(y + n, h, n - 1).wait_recv()
            if n < 3 or h == 1:
                go(pass_down(y + n, h, n))
            go(to_sib(core, n, h))
            ahead(2 * n + h)

    rel_hot[...] = hot(RELS, rels_row[...])
    ra, rb, rc, rd = quarter(relation[...])
    inv = 1.0 / jnp.sqrt(ra * ra + rb * rb + rc * rc + rd * rd)
    scale[...] = inv
    unit[...] = jnp.concatenate([ra * inv, rb * inv, rc * inv, rd * inv], axis=1)
    rot[...] = select(rel_hot[...], unit[...], TN)
    hot_ends[:, pl.ds(0, TRIP)] = hot(N_REL * SLOTS, head_row[...])
    hot_ends[:, pl.ds(TRIP, TRIP)] = hot(N_REL * SLOTS, tail_row[...])

    @pl.loop(1, N_REL)
    def _(k):
        p = lax.rem(rel + k, N_REL)
        rcopy(send_buf.at[p], recv.at[p], a_s.at[k], a_r.at[p], {"rel": p}).wait_recv()

    ends[...] = select(hot_ends[...], recv[...].reshape(N_REL * SLOTS, WIDTH), TN)
    ha, hb, hc, hd = quarter(ends[pl.ds(0, TRIP), :])
    ua, ub, uc, ud = quarter(rot[...])
    qa = ha * ua - hb * ub - hc * uc - hd * ud
    qb = ha * ub + hb * ua + hc * ud - hd * uc
    qc = ha * uc - hb * ud + hc * ua + hd * ub
    qd = ha * ud + hb * uc - hc * ub + hd * ua
    query[...] = jnp.concatenate([qa, qb, qc, qd], axis=1)
    q_hi[...], q_lo[...] = halves(query[...])
    tails = ends[pl.ds(TRIP, TRIP), :]
    positive = jnp.sum(query[...] * tails, axis=1, keepdims=True)
    pull = -1.0 / (1.0 + jnp.exp(positive))
    dq[...] = pull * tails
    dends[pl.ds(TRIP, TRIP), :] = pull * query[...]

    pass_up(y - 4, 0, 3).wait_recv()
    go(to_sib(core, -4, 0))
    pass_down(y + 4, 1, 3).wait_recv()
    go(to_sib(core, -4, 1))
    def score(b):
        q = q_hi[...], q_lo[...]
        n = halves(
            jnp.concatenate(
                [nbuf[b * 4 + w].reshape(ZX * 8, 128) for w in range(4)], axis=1
            )
        )
        s = mm3(q, n, NT)
        p = halves((1.0 / NEGS) / (1.0 + jnp.exp(-s)))
        dq[...] += mm3(p, n, NN)
        dn = mm3(p, q, TN)
        for w in range(4):
            gall[b * 4 + w] = dn[:, w * 128 : w * 128 + 128].reshape(ZX, 8, 128)

    def swap(of, h):
        src = gall.at[pl.ds(of * NY + 4 * h, 4)]
        return rcopy(src, xrecv.at[pl.ds(4 * h, 4)], x_s.at[h], x_r.at[h], sib_dev)

    score(core * 2)
    for off in (0, -1, 1, -2, 2, -3, 3, -4):
        for h in (0, 1):
            to_sib(1 - core, off, h).wait_recv()
    score((1 - core) * 2)
    go(swap(1 - core, 0))
    score((1 - core) * 2 + 1)
    go(swap(1 - core, 1))
    score(core * 2 + 1)

    ga, gb, gc, gd = quarter(dq[...])
    ha, hb, hc, hd = quarter(ends[pl.ds(0, TRIP), :])
    ua, ub, uc, ud = quarter(rot[...])
    dha = ga * ua + gb * ub + gc * uc + gd * ud
    dhb = gb * ua - ga * ub - gc * ud + gd * uc
    dhc = gb * ud - ga * uc + gc * ua - gd * ub
    dhd = gc * ub - ga * ud - gb * uc + gd * ua
    dends[pl.ds(0, TRIP), :] = jnp.concatenate([dha, dhb, dhc, dhd], axis=1)
    gt[...] = select(hot_ends[...], dends[...], NN).reshape(N_REL, SLOTS, WIDTH)

    ret[rel] = gt[rel]
    back(0)
    dua = ga * ha + gb * hb + gc * hc + gd * hd
    dub = gb * ha - ga * hb + gc * hd - gd * hc
    duc = gc * ha - ga * hc - gb * hd + gd * hb
    dud = gb * hc - ga * hd - gc * hb + gd * ha
    du = select(rel_hot[...], jnp.concatenate([dua, dub, duc, dud], axis=1), NN)
    va, vb, vc, vd = quarter(unit[...])
    inv = scale[...]
    da, db, dc, dd = quarter(du)
    along = da * va + db * vb + dc * vc + dd * vd
    parts = [(g - v * along) * inv for g, v in ((da, va), (db, vb), (dc, vc), (dd, vd))]
    for yy in range(NY):
        for g in range(2):
            for w in range(4):
                at = yy * 16 + g * 8
                ring[yy, ZX + g * 4 + w] = parts[w][at : at + 8, :]

    for h in (0, 1):
        swap(core, h).wait_recv()

    @pl.loop(0, NY)
    def _(k):
        ring[k, pl.ds(0, ZX)] = gall[core * NY + k] + xrecv[k]

    def chunk(yy, h):
        return ring.at[lax.rem(yy + 2 * NY, NY), pl.ds(h * CUT, CUT)]

    def take(yy, h, got, n):
        i = lax.rem(yy + 2 * NY, NY)
        cols = pl.ds(h * CUT, CUT)
        ring[i, cols] = ring[i, cols] + got[n, cols]

    def sum_up(yy, h, n):
        at = 2 * n + h
        dst = rp.at[n, pl.ds(h * CUT, CUT)]
        return rcopy(chunk(yy, h), dst, rp_s.at[at], rp_r.at[at], up_dev)

    def sum_down(yy, h, n):
        at = 2 * n + h
        dst = rm.at[n, pl.ds(h * CUT, CUT)]
        return rcopy(chunk(yy, h), dst, rm_s.at[at], rm_r.at[at], down_dev)

    go(sum_up(y + 4, 0, 0))
    go(sum_down(y - 4, 1, 0))
    go(sum_up(y + 3, 1, 1))
    go(sum_down(y - 3, 0, 1))

    for n in (1, 2, 3):
        for h in (1, 0):
            if n > 1 or h == 0:
                sum_up(y + 4 - n, h, n - 1).wait_recv()
                take(y + 4 - n, h, rp, n - 1)
                go(sum_up(y + 4 - n, h, n))
                sum_down(y - 4 + n, 1 - h, n - 1).wait_recv()
                take(y - 4 + n, 1 - h, rm, n - 1)
                go(sum_down(y - 4 + n, 1 - h, n))
                back(2 * n - 1 - h)
    for h in (1, 0):
        sum_up(y, h, 3).wait_recv()
        sum_down(y, 1 - h, 3).wait_recv()
    ring[y] = ring[y] + (rp[3] + rm[3])

    far = {"dom": (1 - zh) * NY + y}
    cross = rcopy(ring.at[y, pl.ds(ZX, 8)], relx, rx_s, rx_r, far)
    go(cross)

    @pl.loop(0, ZX - 1)
    def _(k):
        p = zx_peer(k)
        rcopy(ring.at[y, p], zx_recv.at[zi], z_s.at[k], z_r.at[zi], zx_dev(p)).start()

    back(6)
    zx_recv[zi] = ring[y, zi]

    @pl.loop(0, ZX - 1)
    def _(k):
        p = zx_peer(k)
        rcopy(ring.at[y, p], zx_recv.at[p], z_s.at[k], z_r.at[p], zx_dev(p)).wait_recv()

    tile_out[...] = jnp.sum(zx_recv[...], axis=0)

    @pl.loop(0, N_DOM - 1)
    def _(k):
        p = dom_peer(k)
        rcopy(tile_out, t_recv.at[dom], t_s.at[k], t_r.at[dom], {"dom": p}).start()

    t_recv[dom] = tile_out[...]
    cross.wait_recv()
    rel_full[y] = ring[y, pl.ds(ZX, 8)] + relx[...]

    @pl.loop(1, NY)
    def _(k):
        to = {"dom": zh * NY + lax.rem(y + k, NY)}
        rcopy(rel_full.at[y], rel_full.at[y], ra_s.at[k], ra_r.at[y], to).start()

    @pl.loop(1, N_REL)
    def _(k):
        p = lax.rem(rel + k, N_REL)
        rcopy(gt.at[p], ret.at[p], b_s.at[k], b_r.at[p], {"rel": p}).wait_recv()

    send_hot = hot(ENT, slot_row(send_t))
    grad = select(send_hot, ret[...].reshape(N_REL * SLOTS, WIDTH), NN)

    @pl.loop(0, N_DOM - 1)
    def _(k):
        p = dom_peer(k)
        rcopy(tile_out, t_recv.at[p], t_s.at[k], t_r.at[p], {"dom": p}).wait_recv()

    total = jnp.concatenate(
        [
            jnp.concatenate([t_recv[g * 4 + w] for w in range(4)], axis=1)
            for g in range(4)
        ],
        axis=0,
    )
    owner = jnp.where(neg_part[...] == dom, 1.0, 0.0).astype(F32)
    neg_hot = hot(ENT, neg_rows[pl.ds(rel, 1), :])
    grad_e[...] = grad + owner * select(neg_hot, total, NN)

    @pl.loop(1, NY)
    def _(k):
        i = lax.rem(y + k, NY)
        there = rel_full.at[i]
        rcopy(there, there, ra_s.at[k], ra_r.at[i], {"dom": zh * NY + i}).wait_recv()

    for w in range(4):
        g = jnp.concatenate(
            [rel_full[yy, gg * 4 + w] for yy in range(NY) for gg in range(2)], axis=0
        )
        grad_r[:, pl.ds(w * 128, 128)] = g

    for c in sent:
        c.wait_send()

    @pl.loop(0, N_DOM - 1)
    def _(k):
        p = dom_peer(k)
        rcopy(neg_src.at[p], s1_recv.at[dom], s1_s.at[k], s1_r.at[dom], {"dom": p}).wait_send()
        rcopy(tile_out, t_recv.at[dom], t_s.at[k], t_r.at[dom], {"dom": p}).wait_send()

    @pl.loop(1, N_REL)
    def _(k):
        p = lax.rem(rel + k, N_REL)
        rcopy(send_buf.at[p], recv.at[rel], a_s.at[k], a_r.at[rel], {"rel": p}).wait_send()
        rcopy(gt.at[p], ret.at[rel], b_s.at[k], b_r.at[rel], {"rel": p}).wait_send()

    @pl.loop(0, ZX - 1)
    def _(k):
        p = zx_peer(k)
        here = nbuf.at[mine, zi]
        rcopy(here, here, s2_s.at[k], s2_r.at[zi], zx_dev(p)).wait_send()
        rcopy(ring.at[y, p], zx_recv.at[zi], z_s.at[k], z_r.at[zi], zx_dev(p)).wait_send()

    @pl.loop(1, NY)
    def _(k):
        to = {"dom": zh * NY + lax.rem(y + k, NY)}
        rcopy(rel_full.at[y], rel_full.at[y], ra_s.at[k], ra_r.at[y], to).wait_send()


def shards(
    entity, entity_acc, relation, relation_acc, send_rows, trip_head, trip_rel, trip_tail, neg_part, neg_rows,
):
    send_t = send_rows[0].T
    row = (1, TRIP)
    anywhere = pl.BlockSpec(memory_space=pl.ANY)
    vmem = pl.BlockSpec(memory_space=pltpu.VMEM)
    dma = pltpu.SemaphoreType.DMA
    rows = jax.ShapeDtypeStruct((ENT, WIDTH), F32)
    grad_e, grad_r = pl.pallas_call(
        kernel,
        out_shape=(rows, rows),
        in_specs=[anywhere] * 8,
        out_specs=(vmem, vmem),
        scratch_shapes=[
            pltpu.VMEM((ENT, WIDTH), F32),
            pltpu.VMEM((RELS, WIDTH), F32),
            pltpu.VMEM((SLOTS, N_REL), jnp.int32),
            pltpu.VMEM(row, jnp.int32),
            pltpu.VMEM(row, jnp.int32),
            pltpu.VMEM(row, jnp.int32),
            pltpu.VMEM((N_REL, NEG), jnp.int32),
            pltpu.VMEM((1, 1), jnp.int32),
            pltpu.VMEM((N_REL, SLOTS, WIDTH), F32),
            pltpu.VMEM((N_REL, SLOTS, WIDTH), F32),
            pltpu.VMEM((N_DOM, *TILE), F32),
            pltpu.VMEM((N_DOM, *TILE), F32),
            pltpu.VMEM((2 * NY, ZX, *TILE), F32),
            pltpu.VMEM((N_REL * SLOTS, 2 * TRIP), BF16),
            pltpu.VMEM((2 * TRIP, WIDTH), F32),
            pltpu.VMEM((TRIP, WIDTH), F32),
            pltpu.VMEM((TRIP, WIDTH), F32),
            pltpu.VMEM((TRIP, WIDTH), F32),
            pltpu.VMEM((2 * TRIP, WIDTH), F32),
            pltpu.VMEM((RELS, TRIP), BF16),
            pltpu.VMEM((RELS, WIDTH), F32),
            pltpu.VMEM((RELS, WIDTH // 4), F32),
            pltpu.VMEM((TRIP, WIDTH), BF16),
            pltpu.VMEM((TRIP, WIDTH), BF16),
            pltpu.VMEM((2 * NY, ZX, *TILE), F32),
            pltpu.VMEM((NY, ZX, *TILE), F32),
            pltpu.VMEM((NY, ZX + 8, *TILE), F32),
            pltpu.VMEM((4, ZX + 8, *TILE), F32),
            pltpu.VMEM((4, ZX + 8, *TILE), F32),
            pltpu.VMEM((ZX, *TILE), F32),
            pltpu.VMEM((8, *TILE), F32),
            pltpu.VMEM(TILE, F32),
            pltpu.VMEM((N_DOM, *TILE), F32),
            pltpu.VMEM((NY, 8, *TILE), F32),
            pltpu.VMEM((N_REL, SLOTS, WIDTH), F32),
            pltpu.VMEM((N_REL, SLOTS, WIDTH), F32),
            dma((8,)), dma((N_REL,)), dma((N_REL,)), dma((N_REL,)), dma((N_REL,)),
            dma((N_DOM,)), dma((N_DOM,)), dma((ZX,)), dma((ZX,)),
            dma((8,)), dma((8,)), dma((8,)), dma((8,)),
            dma((16,)), dma((16,)), dma((2,)), dma((2,)),
            dma((8,)), dma((8,)), dma((8,)), dma((8,)),
            dma((ZX,)), dma((ZX,)), dma, dma,
            dma((N_DOM,)), dma((N_DOM,)), dma((NY,)), dma((NY,)),
        ],
        compiler_params=pltpu.CompilerParams(
            collective_id=0, has_side_effects=True, vmem_limit_bytes=56 << 20
        ),
        name="step",
    )(
        entity, relation, send_t, trip_head.reshape(row), trip_tail.reshape(row),
        trip_rel.reshape(row), neg_rows, neg_part.reshape(1, 1),
    )
    return (
        *adagrad(entity, entity_acc, grad_e),
        *adagrad(relation, relation_acc, grad_r),
    )


def solution(mesh):
    both = ("dom", "rel")
    in_specs = (
        P(both, None), P(both, None), P("rel", None), P("rel", None), P(both, None, None),
        P(both), P(both), P(both), P(), P(),
    )
    out_specs = (P(both, None), P(both, None), P("rel", None), P("rel", None))
    return jax.shard_map(shards, mesh=mesh, in_specs=in_specs, out_specs=out_specs, check_vma=False)
```

```python
import jax
import jax.numpy as jnp
from jax import lax
from jax.experimental import pallas as pl
from jax.experimental.pallas import tpu as pltpu
from jax.sharding import PartitionSpec as P

MESH = pl.DeviceIdType.MESH
F32, BF16 = jnp.float32, jnp.bfloat16
step_size = 0.05

N_DOM, N_REL = 16, 32
NY, NX = 8, 4
ZX = 32
ENT, RELS, TRIP, SLOTS, NEG, WIDTH = 128, 128, 256, 16, 32, 512
TILE = (8, 128)
NEGS = NEG * N_REL
AHEAD = (8, 12, 15, 18, 21, 24, 27, 32)
BACK = (9, 12, 14, 16, 18, 20, 32)
HALF = ZX // 2

NN = (((1,), (0,)), ((), ()))
TN = (((0,), (0,)), ((), ()))
NT = (((1,), (1,)), ((), ()))


def mm(a, b, dims):
    return lax.dot_general(a, b, dims, preferred_element_type=F32)


def halves(v):
    hi = v.astype(BF16)
    return hi, (v - hi.astype(F32)).astype(BF16)


def select(one_hot, v, dims):
    hi, lo = halves(v)
    return mm(one_hot, hi, dims) + mm(one_hot, lo, dims)


def mm3(a, b, dims):
    return mm(a[0], b[0], dims) + (mm(a[0], b[1], dims) + mm(a[1], b[0], dims))


def hot(rows, index_row):
    n = index_row.shape[1]
    at = lax.broadcasted_iota(jnp.int32, (rows, n), 0)
    return jnp.where(at == index_row, 1.0, 0.0).astype(BF16)


def slot_row(send_t):
    n = N_REL * SLOTS
    at = lax.broadcasted_iota(jnp.int32, (N_REL, n), 1)
    spread = lax.div(at, SLOTS) == lax.broadcasted_iota(jnp.int32, (N_REL, n), 0)
    full = mm(
        send_t[...].astype(F32).astype(BF16), jnp.where(spread, 1.0, 0.0).astype(BF16), NN
    )
    slot = lax.rem(lax.broadcasted_iota(jnp.int32, (SLOTS, n), 1), SLOTS)
    keep = slot == lax.broadcasted_iota(jnp.int32, (SLOTS, n), 0)
    return jnp.sum(jnp.where(keep, full, 0.0), axis=0, keepdims=True).astype(jnp.int32)


def rcopy(src, dst, ssem, rsem, dev):
    return pltpu.make_async_remote_copy(
        src_ref=src, dst_ref=dst, send_sem=ssem, recv_sem=rsem, device_id=dev, device_id_type=MESH
    )


def quarter(v):
    return v[:, 0:128], v[:, 128:256], v[:, 256:384], v[:, 384:512]


def adagrad(values, history, gradient):
    history_new = history + gradient * gradient
    return values - step_size * gradient / jnp.sqrt(history_new), history_new


def kernel(
    entity_h, relation_h, send_h, head_h, tail_h, rels_h, neg_h, part_h,
    grad_e, grad_r,
    entity, relation, send_t, head_row, tail_row, rels_row, neg_rows, neg_part,
    send_buf, recv, neg_src, s1_recv, nbuf, hot_ends, ends, rot, query, dq, dends,
    rel_hot, unit, scale, q_hi, q_lo, rring, rrp, rrm,
    gall, xrecv, ring, rp, rm, zx_recv, relx, tile_out, t_recv, rel_full, gt, ret,
    in_s, a_s, a_r, b_s, b_r, s1_s, s1_r, s2_s, s2_r, yp_s, yp_r, ym_s, ym_r, sib_s, sib_r, x_s, x_r,
    rp_s, rp_r, rm_s, rm_r, z_s, z_r, rx_s, rx_r, t_s, t_r, ra_s, ra_r,
    up_s, up_r, dn_s, dn_r,
):
    loads = [
        pltpu.make_async_copy(h, v, in_s.at[n])
        for n, (h, v) in enumerate(
            (
                (entity_h, entity), (neg_h, neg_rows), (send_h, send_t), (part_h, neg_part),
                (head_h, head_row), (tail_h, tail_row), (rels_h, rels_row), (relation_h, relation),
            )
        )
    ]
    for c in loads:
        c.start()
    dom, rel = lax.axis_index("dom"), lax.axis_index("rel")
    zh, y = lax.div(dom, NY), lax.rem(dom, NY)
    zx_low, core = lax.div(rel, 2), lax.rem(rel, 2)
    zi = zh * 16 + zx_low
    up, down = lax.rem(y + 1, NY), lax.rem(y + NY - 1, NY)
    up_dev, down_dev = {"dom": zh * NY + up}, {"dom": zh * NY + down}
    sib_dev = {"rel": zx_low * 2 + (1 - core)}

    def zx_dev(p):
        return {"dom": lax.div(p, 16) * NY + y, "rel": lax.rem(p, 16) * 2 + core}

    def fan(j, n):
        return n // 2 + lax.div(j + 1, 2) * (1 - 2 * lax.rem(j, 2))

    def zx_peer(j):
        return lax.rem(zi + fan(j, ZX), ZX)

    def dom_peer(j):
        other = lax.rem(zh + 1 - lax.div(j, NY), 2)
        return other * NY + lax.rem(y + fan(lax.rem(j, NY), NY), NY)

    barrier = pltpu.get_barrier_semaphore()

    @pl.loop(0, N_DOM - 1)
    def _(k):
        pl.semaphore_signal(
            barrier, inc=1, device_id={"dom": dom_peer(k)}, device_id_type=MESH
        )

    @pl.loop(1, N_REL)
    def _(k):
        pl.semaphore_signal(
            barrier, inc=1, device_id={"rel": lax.rem(rel + k, N_REL)}, device_id_type=MESH
        )

    @pl.loop(1, 16)
    def _(k):
        p = (1 - zh) * 16 + lax.rem(zx_low + k, 16)
        pl.semaphore_signal(barrier, inc=1, device_id=zx_dev(p), device_id_type=MESH)

    for c in loads[:4]:
        c.wait()
    ent = halves(entity[...])
    neg_hot = hot(ENT, neg_rows[pl.ds(rel, 1), :])
    own = mm(neg_hot, ent[0], TN) + mm(neg_hot, ent[1], TN)
    for g in range(4):
        for w in range(4):
            neg_src[g * 4 + w] = own[g * 8 : g * 8 + 8, w * 128 : w * 128 + 128]
    send_hot = hot(ENT, slot_row(send_t))
    rows = mm(send_hot, ent[0], TN) + mm(send_hot, ent[1], TN)
    send_buf[...] = rows.reshape(N_REL, SLOTS, WIDTH)
    for c in loads[4:]:
        c.wait()
    is_root = lax.broadcasted_iota(jnp.int32, (N_DOM, 1, 1), 0) == neg_part[...].reshape(1, 1, 1)

    pl.semaphore_wait(barrier, (N_DOM - 1) + (N_REL - 1) + 15)

    @pl.loop(0, N_DOM - 1)
    def _(k):
        p = dom_peer(k)
        rcopy(neg_src.at[p], s1_recv.at[dom], s1_s.at[k], s1_r.at[dom], {"dom": p}).start()

    def peer(k):
        pz = lax.rem(lax.div(rel, 8) + lax.rem(k, 4), 4)
        px = lax.rem(lax.div(lax.rem(rel, 8), 2) + lax.div(k, 8), NX)
        pc = lax.rem(core + lax.rem(lax.div(k, 4), 2), 2)
        return pz * 8 + px * 2 + pc

    def exchange(src, dst, ssem, rsem, lo, hi):
        @pl.loop(lo, hi)
        def _(k):
            p = peer(k)
            rcopy(src.at[p], dst.at[rel], ssem.at[k], rsem.at[rel], {"rel": p}).start()

    def ahead(n):
        exchange(send_buf, recv, a_s, a_r, AHEAD[n - 1] if n else 1, AHEAD[n])

    def back(n):
        exchange(gt, ret, b_s, b_r, BACK[n - 1] if n else 1, BACK[n])

    ahead(0)

    s1_recv[dom] = neg_src[dom]
    recv[rel] = send_buf[rel]

    @pl.loop(0, N_DOM - 1)
    def _(k):
        p = dom_peer(k)
        rcopy(neg_src.at[p], s1_recv.at[p], s1_s.at[k], s1_r.at[p], {"dom": p}).wait_recv()

    mine = core * NY + y
    nbuf[mine, zi] = jnp.sum(jnp.where(is_root, s1_recv[...], 0.0), axis=0)

    @pl.loop(0, ZX - 1)
    def _(k):
        p = zx_peer(k)
        here = nbuf.at[mine, zi]
        rcopy(here, here, s2_s.at[k], s2_r.at[zi], zx_dev(p)).start()

    ahead(1)

    @pl.loop(0, ZX - 1)
    def _(k):
        p = zx_peer(k)
        there = nbuf.at[mine, p]
        rcopy(there, there, s2_s.at[k], s2_r.at[p], zx_dev(p)).wait_recv()

    def part(core_of, yy, h):
        return nbuf.at[core_of * NY + lax.rem(yy + 2 * NY, NY), pl.ds(h * HALF, HALF)]

    def pass_up(yy, h, n):
        ref = part(core, yy, h)
        return rcopy(ref, ref, yp_s.at[2 * n + h], yp_r.at[2 * n + h], up_dev)

    def pass_down(yy, h, n):
        ref = part(core, yy, h)
        return rcopy(ref, ref, ym_s.at[2 * n + h], ym_r.at[2 * n + h], down_dev)

    def to_sib(core_of, off, h):
        ref = part(core_of, y + off, h)
        at = 2 * (off + 4) + h
        return rcopy(ref, ref, sib_s.at[at], sib_r.at[at], sib_dev)

    sent = []

    def go(c):
        c.start()
        sent.append(c)

    for h in (0, 1):
        go(pass_up(y, h, 0))
        go(pass_down(y, h, 0))
    for h in (0, 1):
        go(to_sib(core, 0, h))
    for n in (1, 2, 3):
        for h in (0, 1):
            pass_up(y - n, h, n - 1).wait_recv()
            if n < 3 or h == 0:
                go(pass_up(y - n, h, n))
            go(to_sib(core, -n, h))
            pass_down(y + n, h, n - 1).wait_recv()
            if n < 3 or h == 1:
                go(pass_down(y + n, h, n))
            go(to_sib(core, n, h))
            ahead(2 * n + h)

    rel_hot[...] = hot(RELS, rels_row[...])
    ra, rb, rc, rd = quarter(relation[...])
    inv = 1.0 / jnp.sqrt(ra * ra + rb * rb + rc * rc + rd * rd)
    scale[...] = inv
    unit[...] = jnp.concatenate([ra * inv, rb * inv, rc * inv, rd * inv], axis=1)
    rot[...] = select(rel_hot[...], unit[...], TN)
    hot_ends[:, pl.ds(0, TRIP)] = hot(N_REL * SLOTS, head_row[...])
    hot_ends[:, pl.ds(TRIP, TRIP)] = hot(N_REL * SLOTS, tail_row[...])

    @pl.loop(1, N_REL)
    def _(k):
        p = lax.rem(rel + k, N_REL)
        rcopy(send_buf.at[p], recv.at[p], a_s.at[k], a_r.at[p], {"rel": p}).wait_recv()

    ends[...] = select(hot_ends[...], recv[...].reshape(N_REL * SLOTS, WIDTH), TN)
    ha, hb, hc, hd = quarter(ends[pl.ds(0, TRIP), :])
    ua, ub, uc, ud = quarter(rot[...])
    qa = ha * ua - hb * ub - hc * uc - hd * ud
    qb = ha * ub + hb * ua + hc * ud - hd * uc
    qc = ha * uc - hb * ud + hc * ua + hd * ub
    qd = ha * ud + hb * uc - hc * ub + hd * ua
    query[...] = jnp.concatenate([qa, qb, qc, qd], axis=1)
    q_hi[...], q_lo[...] = halves(query[...])
    tails = ends[pl.ds(TRIP, TRIP), :]
    positive = jnp.sum(query[...] * tails, axis=1, keepdims=True)
    pull = -1.0 / (1.0 + jnp.exp(positive))
    dq[...] = pull * tails
    dends[pl.ds(TRIP, TRIP), :] = pull * query[...]

    pass_up(y - 4, 0, 3).wait_recv()
    go(to_sib(core, -4, 0))
    pass_down(y + 4, 1, 3).wait_recv()
    go(to_sib(core, -4, 1))
    def score(b):
        q = q_hi[...], q_lo[...]
        n = halves(
            jnp.concatenate(
                [nbuf[b * 4 + w].reshape(ZX * 8, 128) for w in range(4)], axis=1
            )
        )
        s = mm3(q, n, NT)
        p = halves((1.0 / NEGS) / (1.0 + jnp.exp(-s)))
        dq[...] += mm3(p, n, NN)
        dn = mm3(p, q, TN)
        for w in range(4):
            gall[b * 4 + w] = dn[:, w * 128 : w * 128 + 128].reshape(ZX, 8, 128)

    def swap(of, h):
        src = gall.at[pl.ds(of * NY + 4 * h, 4)]
        return rcopy(src, xrecv.at[pl.ds(4 * h, 4)], x_s.at[h], x_r.at[h], sib_dev)

    def chunk(yy, h):
        return ring.at[lax.rem(yy + 2 * NY, NY), pl.ds(h * HALF, HALF)]

    def take(yy, h, got, n):
        i = lax.rem(yy + 2 * NY, NY)
        cols = pl.ds(h * HALF, HALF)
        ring[i, cols] = ring[i, cols] + got[n, cols]

    def sum_up(yy, h, n):
        at = 2 * n + h
        dst = rp.at[n, pl.ds(h * HALF, HALF)]
        return rcopy(chunk(yy, h), dst, rp_s.at[at], rp_r.at[at], up_dev)

    def sum_down(yy, h, n):
        at = 2 * n + h
        dst = rm.at[n, pl.ds(h * HALF, HALF)]
        return rcopy(chunk(yy, h), dst, rm_s.at[at], rm_r.at[at], down_dev)

    def neg_step(n, h):
        sum_up(y + 4 - n, h, n - 1).wait_recv()
        take(y + 4 - n, h, rp, n - 1)
        go(sum_up(y + 4 - n, h, n))
        sum_down(y - 4 + n, 1 - h, n - 1).wait_recv()
        take(y - 4 + n, 1 - h, rm, n - 1)
        go(sum_down(y - 4 + n, 1 - h, n))

    def rel_up(n):
        cols = pl.ds(0, 8 if n else 4)
        src = rring.at[lax.rem(y + 4 - n, NY), cols]
        return rcopy(src, rrp.at[n, cols], up_s.at[n], up_r.at[n], up_dev)

    def rel_down(n):
        cols = pl.ds(0, 8) if n else pl.ds(4, 4)
        src = rring.at[lax.rem(y + 4 + n, NY), cols]
        return rcopy(src, rrm.at[n, cols], dn_s.at[n], dn_r.at[n], down_dev)

    def rel_step(n):
        u, d = lax.rem(y + 4 - n, NY), lax.rem(y + 4 + n, NY)
        uc, dc = (pl.ds(0, 4), pl.ds(4, 4)) if n == 1 else (pl.ds(0, 8), pl.ds(0, 8))
        rel_up(n - 1).wait_recv()
        rring[u, uc] = rring[u, uc] + rrp[n - 1, uc]
        go(rel_up(n))
        rel_down(n - 1).wait_recv()
        rring[d, dc] = rring[d, dc] + rrm[n - 1, dc]
        go(rel_down(n))

    def merge(h):
        swap(core, h).wait_recv()

        @pl.loop(0, 4)
        def _(k):
            i = h * 4 + k
            ring[i] = gall[core * NY + i] + xrecv[i]

    near = lax.div(y, 4)
    away = 1 - near
    score(core * 2 + away)
    for off in (0, -1, 1, -2, 2, -3, 3, -4):
        for h in (0, 1):
            to_sib(1 - core, off, h).wait_recv()
    score((1 - core) * 2 + away)
    go(swap(1 - core, away))
    score((1 - core) * 2 + near)
    go(swap(1 - core, near))
    merge(away)
    go(sum_up(y + 4, 0, 0))
    go(sum_down(y - 4, 1, 0))
    score(core * 2 + near)
    merge(near)
    go(sum_up(y + 3, 1, 1))
    go(sum_down(y - 3, 0, 1))

    ga, gb, gc, gd = quarter(dq[...])
    ha, hb, hc, hd = quarter(ends[pl.ds(0, TRIP), :])
    ua, ub, uc, ud = quarter(rot[...])
    dha = ga * ua + gb * ub + gc * uc + gd * ud
    dhb = gb * ua - ga * ub - gc * ud + gd * uc
    dhc = gb * ud - ga * uc + gc * ua - gd * ub
    dhd = gc * ub - ga * ud - gb * uc + gd * ua
    dends[pl.ds(0, TRIP), :] = jnp.concatenate([dha, dhb, dhc, dhd], axis=1)
    gt[...] = select(hot_ends[...], dends[...], NN).reshape(N_REL, SLOTS, WIDTH)

    ret[rel] = gt[rel]
    back(0)
    neg_step(1, 0)
    back(1)
    dua = ga * ha + gb * hb + gc * hc + gd * hd
    dub = gb * ha - ga * hb + gc * hd - gd * hc
    duc = gc * ha - ga * hc - gb * hd + gd * hb
    dud = gb * hc - ga * hd - gc * hb + gd * ha
    du = select(rel_hot[...], jnp.concatenate([dua, dub, duc, dud], axis=1), NN)
    va, vb, vc, vd = quarter(unit[...])
    inv = scale[...]
    da, db, dc, dd = quarter(du)
    along = da * va + db * vb + dc * vc + dd * vd
    parts = [(g - v * along) * inv for g, v in ((da, va), (db, vb), (dc, vc), (dd, vd))]
    for yy in range(NY):
        for g in range(2):
            for w in range(4):
                at = yy * 16 + g * 8
                rring[yy, g * 4 + w] = parts[w][at : at + 8, :]
    go(rel_up(0))
    go(rel_down(0))

    for n in (2, 3):
        for h in (1, 0):
            neg_step(n, h)
            back(2 * n - 1 - h)
        rel_step(n - 1)
    for h in (1, 0):
        sum_up(y, h, 3).wait_recv()
        sum_down(y, 1 - h, 3).wait_recv()
    ring[y] = ring[y] + (rp[3] + rm[3])

    far = {"dom": (1 - zh) * NY + y}
    cross = rcopy(rring.at[y], relx, rx_s, rx_r, far)

    @pl.loop(0, ZX - 1)
    def _(k):
        p = zx_peer(k)
        rcopy(ring.at[y, p], zx_recv.at[zi], z_s.at[k], z_r.at[zi], zx_dev(p)).start()

    rel_step(3)
    rel_up(3).wait_recv()
    rel_down(3).wait_recv()
    rring[y] = rring[y] + (rrp[3] + rrm[3])
    go(cross)
    back(6)
    zx_recv[zi] = ring[y, zi]

    @pl.loop(0, ZX - 1)
    def _(k):
        p = zx_peer(k)
        rcopy(ring.at[y, p], zx_recv.at[p], z_s.at[k], z_r.at[p], zx_dev(p)).wait_recv()

    tile_out[...] = jnp.sum(zx_recv[...], axis=0)

    @pl.loop(0, N_DOM - 1)
    def _(k):
        p = dom_peer(k)
        rcopy(tile_out, t_recv.at[dom], t_s.at[k], t_r.at[dom], {"dom": p}).start()

    t_recv[dom] = tile_out[...]
    cross.wait_recv()
    rel_full[y] = rring[y] + relx[...]

    @pl.loop(1, NY)
    def _(k):
        to = {"dom": zh * NY + lax.rem(y + k, NY)}
        rcopy(rel_full.at[y], rel_full.at[y], ra_s.at[k], ra_r.at[y], to).start()

    @pl.loop(1, N_REL)
    def _(k):
        p = lax.rem(rel + k, N_REL)
        rcopy(gt.at[p], ret.at[p], b_s.at[k], b_r.at[p], {"rel": p}).wait_recv()

    send_hot = hot(ENT, slot_row(send_t))
    grad = select(send_hot, ret[...].reshape(N_REL * SLOTS, WIDTH), NN)

    @pl.loop(0, N_DOM - 1)
    def _(k):
        p = dom_peer(k)
        rcopy(tile_out, t_recv.at[p], t_s.at[k], t_r.at[p], {"dom": p}).wait_recv()

    total = jnp.concatenate(
        [
            jnp.concatenate([t_recv[g * 4 + w] for w in range(4)], axis=1)
            for g in range(4)
        ],
        axis=0,
    )
    owner = jnp.where(neg_part[...] == dom, 1.0, 0.0).astype(F32)
    neg_hot = hot(ENT, neg_rows[pl.ds(rel, 1), :])
    grad_e[...] = grad + owner * select(neg_hot, total, NN)

    @pl.loop(1, NY)
    def _(k):
        i = lax.rem(y + k, NY)
        there = rel_full.at[i]
        rcopy(there, there, ra_s.at[k], ra_r.at[i], {"dom": zh * NY + i}).wait_recv()

    for w in range(4):
        g = jnp.concatenate(
            [rel_full[yy, gg * 4 + w] for yy in range(NY) for gg in range(2)], axis=0
        )
        grad_r[:, pl.ds(w * 128, 128)] = g

    for c in sent:
        c.wait_send()

    @pl.loop(0, N_DOM - 1)
    def _(k):
        p = dom_peer(k)
        rcopy(neg_src.at[p], s1_recv.at[dom], s1_s.at[k], s1_r.at[dom], {"dom": p}).wait_send()
        rcopy(tile_out, t_recv.at[dom], t_s.at[k], t_r.at[dom], {"dom": p}).wait_send()

    @pl.loop(1, N_REL)
    def _(k):
        p = lax.rem(rel + k, N_REL)
        rcopy(send_buf.at[p], recv.at[rel], a_s.at[k], a_r.at[rel], {"rel": p}).wait_send()
        rcopy(gt.at[p], ret.at[rel], b_s.at[k], b_r.at[rel], {"rel": p}).wait_send()

    @pl.loop(0, ZX - 1)
    def _(k):
        p = zx_peer(k)
        here = nbuf.at[mine, zi]
        rcopy(here, here, s2_s.at[k], s2_r.at[zi], zx_dev(p)).wait_send()
        rcopy(ring.at[y, p], zx_recv.at[zi], z_s.at[k], z_r.at[zi], zx_dev(p)).wait_send()

    @pl.loop(1, NY)
    def _(k):
        to = {"dom": zh * NY + lax.rem(y + k, NY)}
        rcopy(rel_full.at[y], rel_full.at[y], ra_s.at[k], ra_r.at[y], to).wait_send()


def shards(
    entity, entity_acc, relation, relation_acc, send_rows, trip_head, trip_rel, trip_tail, neg_part, neg_rows,
):
    send_t = send_rows[0].T
    row = (1, TRIP)
    anywhere = pl.BlockSpec(memory_space=pl.ANY)
    vmem = pl.BlockSpec(memory_space=pltpu.VMEM)
    dma = pltpu.SemaphoreType.DMA
    rows = jax.ShapeDtypeStruct((ENT, WIDTH), F32)
    grad_e, grad_r = pl.pallas_call(
        kernel,
        out_shape=(rows, rows),
        in_specs=[anywhere] * 8,
        out_specs=(vmem, vmem),
        scratch_shapes=[
            pltpu.VMEM((ENT, WIDTH), F32),
            pltpu.VMEM((RELS, WIDTH), F32),
            pltpu.VMEM((SLOTS, N_REL), jnp.int32),
            pltpu.VMEM(row, jnp.int32),
            pltpu.VMEM(row, jnp.int32),
            pltpu.VMEM(row, jnp.int32),
            pltpu.VMEM((N_REL, NEG), jnp.int32),
            pltpu.VMEM((1, 1), jnp.int32),
            pltpu.VMEM((N_REL, SLOTS, WIDTH), F32),
            pltpu.VMEM((N_REL, SLOTS, WIDTH), F32),
            pltpu.VMEM((N_DOM, *TILE), F32),
            pltpu.VMEM((N_DOM, *TILE), F32),
            pltpu.VMEM((2 * NY, ZX, *TILE), F32),
            pltpu.VMEM((N_REL * SLOTS, 2 * TRIP), BF16),
            pltpu.VMEM((2 * TRIP, WIDTH), F32),
            pltpu.VMEM((TRIP, WIDTH), F32),
            pltpu.VMEM((TRIP, WIDTH), F32),
            pltpu.VMEM((TRIP, WIDTH), F32),
            pltpu.VMEM((2 * TRIP, WIDTH), F32),
            pltpu.VMEM((RELS, TRIP), BF16),
            pltpu.VMEM((RELS, WIDTH), F32),
            pltpu.VMEM((RELS, WIDTH // 4), F32),
            pltpu.VMEM((TRIP, WIDTH), BF16),
            pltpu.VMEM((TRIP, WIDTH), BF16),
            pltpu.VMEM((NY, 8, *TILE), F32),
            pltpu.VMEM((4, 8, *TILE), F32),
            pltpu.VMEM((4, 8, *TILE), F32),
            pltpu.VMEM((2 * NY, ZX, *TILE), F32),
            pltpu.VMEM((NY, ZX, *TILE), F32),
            pltpu.VMEM((NY, ZX, *TILE), F32),
            pltpu.VMEM((4, ZX, *TILE), F32),
            pltpu.VMEM((4, ZX, *TILE), F32),
            pltpu.VMEM((ZX, *TILE), F32),
            pltpu.VMEM((8, *TILE), F32),
            pltpu.VMEM(TILE, F32),
            pltpu.VMEM((N_DOM, *TILE), F32),
            pltpu.VMEM((NY, 8, *TILE), F32),
            pltpu.VMEM((N_REL, SLOTS, WIDTH), F32),
            pltpu.VMEM((N_REL, SLOTS, WIDTH), F32),
            dma((8,)), dma((N_REL,)), dma((N_REL,)), dma((N_REL,)), dma((N_REL,)),
            dma((N_DOM,)), dma((N_DOM,)), dma((ZX,)), dma((ZX,)),
            dma((8,)), dma((8,)), dma((8,)), dma((8,)),
            dma((16,)), dma((16,)), dma((2,)), dma((2,)),
            dma((8,)), dma((8,)), dma((8,)), dma((8,)),
            dma((ZX,)), dma((ZX,)), dma, dma,
            dma((N_DOM,)), dma((N_DOM,)), dma((NY,)), dma((NY,)),
            dma((4,)), dma((4,)), dma((4,)), dma((4,)),
        ],
        compiler_params=pltpu.CompilerParams(
            collective_id=0, has_side_effects=True, vmem_limit_bytes=56 << 20
        ),
        name="step",
    )(
        entity, relation, send_t, trip_head.reshape(row), trip_tail.reshape(row),
        trip_rel.reshape(row), neg_rows, neg_part.reshape(1, 1),
    )
    return (
        *adagrad(entity, entity_acc, grad_e),
        *adagrad(relation, relation_acc, grad_r),
    )


def solution(mesh):
    both = ("dom", "rel")
    in_specs = (
        P(both, None), P(both, None), P("rel", None), P("rel", None), P(both, None, None),
        P(both), P(both), P(both), P(), P(),
    )
    out_specs = (P(both, None), P(both, None), P("rel", None), P("rel", None))
    return jax.shard_map(shards, mesh=mesh, in_specs=in_specs, out_specs=out_specs, check_vma=False)
```

```python
import jax
import jax.numpy as jnp
from jax import lax
from jax.experimental import pallas as pl
from jax.experimental.pallas import tpu as pltpu
from jax.sharding import PartitionSpec as P

MESH = pl.DeviceIdType.MESH
F32, BF16 = jnp.float32, jnp.bfloat16
step_size = 0.05

N_DOM, N_REL = 16, 32
NY, NX = 8, 4
ZX = 32
ENT, RELS, TRIP, SLOTS, NEG, WIDTH = 128, 128, 256, 16, 32, 512
TILE = (8, 128)
NEGS = NEG * N_REL
AHEAD = (8, 12, 15, 18, 21, 24, 27, 32)
BACK = (9, 12, 14, 16, 18, 20, 32)
HALF = ZX // 2

NN = (((1,), (0,)), ((), ()))
TN = (((0,), (0,)), ((), ()))
NT = (((1,), (1,)), ((), ()))


def mm(a, b, dims):
    return lax.dot_general(a, b, dims, preferred_element_type=F32)


def halves(v):
    hi = v.astype(BF16)
    return hi, (v - hi.astype(F32)).astype(BF16)


def select(one_hot, v, dims):
    hi, lo = halves(v)
    return mm(one_hot, hi, dims) + mm(one_hot, lo, dims)


def mm3(a, b, dims):
    return mm(a[0], b[0], dims) + (mm(a[0], b[1], dims) + mm(a[1], b[0], dims))


def hot(rows, index_row):
    n = index_row.shape[1]
    at = lax.broadcasted_iota(jnp.int32, (rows, n), 0)
    return jnp.where(at == index_row, 1.0, 0.0).astype(BF16)


def slot_row(send_t):
    n = N_REL * SLOTS
    at = lax.broadcasted_iota(jnp.int32, (N_REL, n), 1)
    spread = lax.div(at, SLOTS) == lax.broadcasted_iota(jnp.int32, (N_REL, n), 0)
    full = mm(
        send_t[...].astype(F32).astype(BF16), jnp.where(spread, 1.0, 0.0).astype(BF16), NN
    )
    slot = lax.rem(lax.broadcasted_iota(jnp.int32, (SLOTS, n), 1), SLOTS)
    keep = slot == lax.broadcasted_iota(jnp.int32, (SLOTS, n), 0)
    return jnp.sum(jnp.where(keep, full, 0.0), axis=0, keepdims=True).astype(jnp.int32)


def rcopy(src, dst, ssem, rsem, dev):
    return pltpu.make_async_remote_copy(
        src_ref=src, dst_ref=dst, send_sem=ssem, recv_sem=rsem, device_id=dev, device_id_type=MESH
    )


def quarter(v):
    return v[:, 0:128], v[:, 128:256], v[:, 256:384], v[:, 384:512]


def adagrad(values, history, gradient):
    history_new = history + gradient * gradient
    return values - step_size * gradient / jnp.sqrt(history_new), history_new


def kernel(
    entity_h, relation_h, send_h, head_h, tail_h, rels_h, neg_h, part_h,
    grad_e, grad_r,
    entity, relation, send_t, head_row, tail_row, rels_row, neg_rows, neg_part,
    send_buf, recv, neg_src, s1_recv, nbuf, hot_ends, ends, rot, query, dq, dends,
    rel_hot, unit, scale, q_hi, q_lo, rring, rrp, rrm,
    gall, xrecv, ring, rp, rm, zx_recv, relx, cand, far_recv, t_recv, rel_full, gt, ret,
    in_s, a_s, a_r, b_s, b_r, s1_s, s1_r, s2_s, s2_r, yp_s, yp_r, ym_s, ym_r, sib_s, sib_r, x_s, x_r,
    rp_s, rp_r, rm_s, rm_r, z_s, z_r, rx_s, rx_r, t_s, t_r, ra_s, ra_r,
    up_s, up_r, dn_s, dn_r, f_s, f_r,
):
    loads = [
        pltpu.make_async_copy(h, v, in_s.at[n])
        for n, (h, v) in enumerate(
            (
                (entity_h, entity), (neg_h, neg_rows), (send_h, send_t), (part_h, neg_part),
                (head_h, head_row), (tail_h, tail_row), (rels_h, rels_row), (relation_h, relation),
            )
        )
    ]
    for c in loads:
        c.start()
    dom, rel = lax.axis_index("dom"), lax.axis_index("rel")
    zh, y = lax.div(dom, NY), lax.rem(dom, NY)
    zx_low, core = lax.div(rel, 2), lax.rem(rel, 2)
    zi = zh * 16 + zx_low
    up, down = lax.rem(y + 1, NY), lax.rem(y + NY - 1, NY)
    up_dev, down_dev = {"dom": zh * NY + up}, {"dom": zh * NY + down}
    sib_dev = {"rel": zx_low * 2 + (1 - core)}

    def zx_dev(p):
        return {"dom": lax.div(p, 16) * NY + y, "rel": lax.rem(p, 16) * 2 + core}

    def fan(j, n):
        return n // 2 + lax.div(j + 1, 2) * (1 - 2 * lax.rem(j, 2))

    def zx_peer(j):
        return lax.rem(zi + fan(j, ZX), ZX)

    def y_peer(j):
        return lax.rem(y + fan(j, NY), NY)

    far = {"dom": (1 - zh) * NY + y}

    barrier = pltpu.get_barrier_semaphore()

    @pl.loop(0, NY - 1)
    def _(k):
        to = {"dom": zh * NY + y_peer(k)}
        pl.semaphore_signal(barrier, inc=1, device_id=to, device_id_type=MESH)

    @pl.loop(1, N_REL)
    def _(k):
        pl.semaphore_signal(
            barrier, inc=1, device_id={"rel": lax.rem(rel + k, N_REL)}, device_id_type=MESH
        )

    @pl.loop(0, 16)
    def _(k):
        p = (1 - zh) * 16 + lax.rem(zx_low + k, 16)
        pl.semaphore_signal(barrier, inc=1, device_id=zx_dev(p), device_id_type=MESH)

    for c in loads[:4]:
        c.wait()
    ent = halves(entity[...])
    neg_hot = hot(ENT, neg_rows[pl.ds(rel, 1), :])
    own = mm(neg_hot, ent[0], TN) + mm(neg_hot, ent[1], TN)
    for g in range(4):
        for w in range(4):
            neg_src[(g % 2) * 4 + w, g // 2] = own[g * 8 : g * 8 + 8, w * 128 : w * 128 + 128]
    send_hot = hot(ENT, slot_row(send_t))
    rows = mm(send_hot, ent[0], TN) + mm(send_hot, ent[1], TN)
    send_buf[...] = rows.reshape(N_REL, SLOTS, WIDTH)
    for c in loads[4:]:
        c.wait()
    root_y = lax.rem(neg_part[...], NY).reshape(1, 1, 1, 1)
    is_root = lax.broadcasted_iota(jnp.int32, (NY, 1, 1, 1), 0) == root_y

    pl.semaphore_wait(barrier, (NY - 1) + (N_REL - 1) + 16)

    def scatter(k, slot):
        p = y_peer(k)
        at = y if slot is None else p
        return rcopy(
            neg_src.at[p], s1_recv.at[at], s1_s.at[k], s1_r.at[at], {"dom": zh * NY + p}
        )

    @pl.loop(0, NY - 1)
    def _(k):
        scatter(k, None).start()

    sent = []

    def go(c):
        c.start()
        sent.append(c)

    def peer(k):
        pz = lax.rem(lax.div(rel, 8) + lax.rem(k, 4), 4)
        px = lax.rem(lax.div(lax.rem(rel, 8), 2) + lax.div(k, 8), NX)
        pc = lax.rem(core + lax.rem(lax.div(k, 4), 2), 2)
        return pz * 8 + px * 2 + pc

    def exchange(src, dst, ssem, rsem, lo, hi):
        @pl.loop(lo, hi)
        def _(k):
            p = peer(k)
            rcopy(src.at[p], dst.at[rel], ssem.at[k], rsem.at[rel], {"rel": p}).start()

    def ahead(n):
        exchange(send_buf, recv, a_s, a_r, AHEAD[n - 1] if n else 1, AHEAD[n])

    def back(n):
        exchange(gt, ret, b_s, b_r, BACK[n - 1] if n else 1, BACK[n])

    ahead(0)

    s1_recv[y] = neg_src[y]
    recv[rel] = send_buf[rel]

    @pl.loop(0, NY - 1)
    def _(k):
        scatter(k, 0).wait_recv()

    cand[...] = jnp.sum(jnp.where(is_root, s1_recv[...], 0.0), axis=0)
    over = rcopy(cand.at[1 - zh], far_recv, f_s.at[0], f_r.at[0], far)
    go(over)
    over.wait_recv()
    mine = core * NY + y
    here = lax.div(neg_part[...], NY) == zh
    nbuf[mine, zi] = jnp.where(here, cand[zh], far_recv[...])

    @pl.loop(0, ZX - 1)
    def _(k):
        p = zx_peer(k)
        here = nbuf.at[mine, zi]
        rcopy(here, here, s2_s.at[k], s2_r.at[zi], zx_dev(p)).start()

    ahead(1)

    @pl.loop(0, ZX - 1)
    def _(k):
        p = zx_peer(k)
        there = nbuf.at[mine, p]
        rcopy(there, there, s2_s.at[k], s2_r.at[p], zx_dev(p)).wait_recv()

    def part(core_of, yy, h):
        return nbuf.at[core_of * NY + lax.rem(yy + 2 * NY, NY), pl.ds(h * HALF, HALF)]

    def pass_up(yy, h, n):
        ref = part(core, yy, h)
        return rcopy(ref, ref, yp_s.at[2 * n + h], yp_r.at[2 * n + h], up_dev)

    def pass_down(yy, h, n):
        ref = part(core, yy, h)
        return rcopy(ref, ref, ym_s.at[2 * n + h], ym_r.at[2 * n + h], down_dev)

    def to_sib(core_of, off, h):
        ref = part(core_of, y + off, h)
        at = 2 * (off + 4) + h
        return rcopy(ref, ref, sib_s.at[at], sib_r.at[at], sib_dev)

    for h in (0, 1):
        go(pass_up(y, h, 0))
        go(pass_down(y, h, 0))
    for h in (0, 1):
        go(to_sib(core, 0, h))
    for n in (1, 2, 3):
        for h in (0, 1):
            pass_up(y - n, h, n - 1).wait_recv()
            if n < 3 or h == 0:
                go(pass_up(y - n, h, n))
            go(to_sib(core, -n, h))
            pass_down(y + n, h, n - 1).wait_recv()
            if n < 3 or h == 1:
                go(pass_down(y + n, h, n))
            go(to_sib(core, n, h))
            ahead(2 * n + h)

    rel_hot[...] = hot(RELS, rels_row[...])
    ra, rb, rc, rd = quarter(relation[...])
    inv = 1.0 / jnp.sqrt(ra * ra + rb * rb + rc * rc + rd * rd)
    scale[...] = inv
    unit[...] = jnp.concatenate([ra * inv, rb * inv, rc * inv, rd * inv], axis=1)
    rot[...] = select(rel_hot[...], unit[...], TN)
    hot_ends[:, pl.ds(0, TRIP)] = hot(N_REL * SLOTS, head_row[...])
    hot_ends[:, pl.ds(TRIP, TRIP)] = hot(N_REL * SLOTS, tail_row[...])

    @pl.loop(1, N_REL)
    def _(k):
        p = lax.rem(rel + k, N_REL)
        rcopy(send_buf.at[p], recv.at[p], a_s.at[k], a_r.at[p], {"rel": p}).wait_recv()

    ends[...] = select(hot_ends[...], recv[...].reshape(N_REL * SLOTS, WIDTH), TN)
    ha, hb, hc, hd = quarter(ends[pl.ds(0, TRIP), :])
    ua, ub, uc, ud = quarter(rot[...])
    qa = ha * ua - hb * ub - hc * uc - hd * ud
    qb = ha * ub + hb * ua + hc * ud - hd * uc
    qc = ha * uc - hb * ud + hc * ua + hd * ub
    qd = ha * ud + hb * uc - hc * ub + hd * ua
    query[...] = jnp.concatenate([qa, qb, qc, qd], axis=1)
    q_hi[...], q_lo[...] = halves(query[...])
    tails = ends[pl.ds(TRIP, TRIP), :]
    positive = jnp.sum(query[...] * tails, axis=1, keepdims=True)
    pull = -1.0 / (1.0 + jnp.exp(positive))
    dq[...] = pull * tails
    dends[pl.ds(TRIP, TRIP), :] = pull * query[...]

    pass_up(y - 4, 0, 3).wait_recv()
    go(to_sib(core, -4, 0))
    pass_down(y + 4, 1, 3).wait_recv()
    go(to_sib(core, -4, 1))
    def score(b):
        q = q_hi[...], q_lo[...]
        n = halves(
            jnp.concatenate(
                [nbuf[b * 4 + w].reshape(ZX * 8, 128) for w in range(4)], axis=1
            )
        )
        s = mm3(q, n, NT)
        p = halves((1.0 / NEGS) / (1.0 + jnp.exp(-s)))
        dq[...] += mm3(p, n, NN)
        dn = mm3(p, q, TN)
        for w in range(4):
            gall[b * 4 + w] = dn[:, w * 128 : w * 128 + 128].reshape(ZX, 8, 128)

    def swap(of, h):
        src = gall.at[pl.ds(of * NY + 4 * h, 4)]
        return rcopy(src, xrecv.at[pl.ds(4 * h, 4)], x_s.at[h], x_r.at[h], sib_dev)

    def chunk(yy, h):
        return ring.at[lax.rem(yy + 2 * NY, NY), pl.ds(h * HALF, HALF)]

    def take(yy, h, got, n):
        i = lax.rem(yy + 2 * NY, NY)
        cols = pl.ds(h * HALF, HALF)
        ring[i, cols] = ring[i, cols] + got[n, cols]

    def sum_up(yy, h, n):
        at = 2 * n + h
        dst = rp.at[n, pl.ds(h * HALF, HALF)]
        return rcopy(chunk(yy, h), dst, rp_s.at[at], rp_r.at[at], up_dev)

    def sum_down(yy, h, n):
        at = 2 * n + h
        dst = rm.at[n, pl.ds(h * HALF, HALF)]
        return rcopy(chunk(yy, h), dst, rm_s.at[at], rm_r.at[at], down_dev)

    def neg_step(n, h):
        sum_up(y + 4 - n, h, n - 1).wait_recv()
        take(y + 4 - n, h, rp, n - 1)
        go(sum_up(y + 4 - n, h, n))
        sum_down(y - 4 + n, 1 - h, n - 1).wait_recv()
        take(y - 4 + n, 1 - h, rm, n - 1)
        go(sum_down(y - 4 + n, 1 - h, n))

    def rel_up(n):
        cols = pl.ds(0, 8 if n else 4)
        src = rring.at[lax.rem(y + 4 - n, NY), cols]
        return rcopy(src, rrp.at[n, cols], up_s.at[n], up_r.at[n], up_dev)

    def rel_down(n):
        cols = pl.ds(0, 8) if n else pl.ds(4, 4)
        src = rring.at[lax.rem(y + 4 + n, NY), cols]
        return rcopy(src, rrm.at[n, cols], dn_s.at[n], dn_r.at[n], down_dev)

    def rel_step(n):
        u, d = lax.rem(y + 4 - n, NY), lax.rem(y + 4 + n, NY)
        uc, dc = (pl.ds(0, 4), pl.ds(4, 4)) if n == 1 else (pl.ds(0, 8), pl.ds(0, 8))
        rel_up(n - 1).wait_recv()
        rring[u, uc] = rring[u, uc] + rrp[n - 1, uc]
        go(rel_up(n))
        rel_down(n - 1).wait_recv()
        rring[d, dc] = rring[d, dc] + rrm[n - 1, dc]
        go(rel_down(n))

    def merge(h):
        swap(core, h).wait_recv()

        @pl.loop(0, 4)
        def _(k):
            i = h * 4 + k
            ring[i] = gall[core * NY + i] + xrecv[i]

    near = lax.div(y, 4)
    away = 1 - near
    score(core * 2 + away)
    for off in (0, -1, 1, -2, 2, -3, 3, -4):
        for h in (0, 1):
            to_sib(1 - core, off, h).wait_recv()
    score((1 - core) * 2 + away)
    go(swap(1 - core, away))
    score((1 - core) * 2 + near)
    go(swap(1 - core, near))
    merge(away)
    go(sum_up(y + 4, 0, 0))
    go(sum_down(y - 4, 1, 0))
    score(core * 2 + near)
    merge(near)
    go(sum_up(y + 3, 1, 1))
    go(sum_down(y - 3, 0, 1))

    ga, gb, gc, gd = quarter(dq[...])
    ha, hb, hc, hd = quarter(ends[pl.ds(0, TRIP), :])
    ua, ub, uc, ud = quarter(rot[...])
    dha = ga * ua + gb * ub + gc * uc + gd * ud
    dhb = gb * ua - ga * ub - gc * ud + gd * uc
    dhc = gb * ud - ga * uc + gc * ua - gd * ub
    dhd = gc * ub - ga * ud - gb * uc + gd * ua
    dends[pl.ds(0, TRIP), :] = jnp.concatenate([dha, dhb, dhc, dhd], axis=1)
    gt[...] = select(hot_ends[...], dends[...], NN).reshape(N_REL, SLOTS, WIDTH)

    ret[rel] = gt[rel]
    back(0)
    neg_step(1, 0)
    back(1)
    dua = ga * ha + gb * hb + gc * hc + gd * hd
    dub = gb * ha - ga * hb + gc * hd - gd * hc
    duc = gc * ha - ga * hc - gb * hd + gd * hb
    dud = gb * hc - ga * hd - gc * hb + gd * ha
    du = select(rel_hot[...], jnp.concatenate([dua, dub, duc, dud], axis=1), NN)
    va, vb, vc, vd = quarter(unit[...])
    inv = scale[...]
    da, db, dc, dd = quarter(du)
    along = da * va + db * vb + dc * vc + dd * vd
    parts = [(g - v * along) * inv for g, v in ((da, va), (db, vb), (dc, vc), (dd, vd))]
    for yy in range(NY):
        for g in range(2):
            for w in range(4):
                at = yy * 16 + g * 8
                rring[yy, g * 4 + w] = parts[w][at : at + 8, :]
    go(rel_up(0))
    go(rel_down(0))

    for n in (2, 3):
        for h in (1, 0):
            neg_step(n, h)
            back(2 * n - 1 - h)
        rel_step(n - 1)
    for h in (1, 0):
        sum_up(y, h, 3).wait_recv()
        sum_down(y, 1 - h, 3).wait_recv()
    ring[y] = ring[y] + (rp[3] + rm[3])

    cross = rcopy(rring.at[y], relx, rx_s, rx_r, far)

    @pl.loop(0, ZX - 1)
    def _(k):
        p = zx_peer(k)
        rcopy(ring.at[y, p], zx_recv.at[zi], z_s.at[k], z_r.at[zi], zx_dev(p)).start()

    rel_step(3)
    rel_up(3).wait_recv()
    rel_down(3).wait_recv()
    rring[y] = rring[y] + (rrp[3] + rrm[3])
    go(cross)
    back(6)
    zx_recv[zi] = ring[y, zi]

    @pl.loop(0, ZX - 1)
    def _(k):
        p = zx_peer(k)
        rcopy(ring.at[y, p], zx_recv.at[p], z_s.at[k], z_r.at[p], zx_dev(p)).wait_recv()

    t_recv[y, zh] = jnp.sum(zx_recv[...], axis=0)
    go(rcopy(t_recv.at[y, zh], t_recv.at[y, zh], f_s.at[1], f_r.at[1], far))
    cross.wait_recv()
    rel_full[y] = rring[y] + relx[...]

    @pl.loop(1, NY)
    def _(k):
        to = {"dom": zh * NY + lax.rem(y + k, NY)}
        rcopy(rel_full.at[y], rel_full.at[y], ra_s.at[k], ra_r.at[y], to).start()

    there = t_recv.at[y, 1 - zh]
    rcopy(there, there, f_s.at[1], f_r.at[1], far).wait_recv()

    def gather(k, slot):
        p = y_peer(k)
        at = y if slot is None else p
        return rcopy(
            t_recv.at[at], t_recv.at[at], t_s.at[k], t_r.at[at], {"dom": zh * NY + p}
        )

    @pl.loop(0, NY - 1)
    def _(k):
        gather(k, None).start()

    @pl.loop(1, N_REL)
    def _(k):
        p = lax.rem(rel + k, N_REL)
        rcopy(gt.at[p], ret.at[p], b_s.at[k], b_r.at[p], {"rel": p}).wait_recv()

    send_hot = hot(ENT, slot_row(send_t))
    grad = select(send_hot, ret[...].reshape(N_REL * SLOTS, WIDTH), NN)

    @pl.loop(0, NY - 1)
    def _(k):
        gather(k, 0).wait_recv()

    total = jnp.concatenate(
        [
            jnp.concatenate([t_recv[(g % 2) * 4 + w, g // 2] for w in range(4)], axis=1)
            for g in range(4)
        ],
        axis=0,
    )
    owner = jnp.where(neg_part[...] == dom, 1.0, 0.0).astype(F32)
    neg_hot = hot(ENT, neg_rows[pl.ds(rel, 1), :])
    grad_e[...] = grad + owner * select(neg_hot, total, NN)

    @pl.loop(1, NY)
    def _(k):
        i = lax.rem(y + k, NY)
        there = rel_full.at[i]
        rcopy(there, there, ra_s.at[k], ra_r.at[i], {"dom": zh * NY + i}).wait_recv()

    for w in range(4):
        g = jnp.concatenate(
            [rel_full[yy, gg * 4 + w] for yy in range(NY) for gg in range(2)], axis=0
        )
        grad_r[:, pl.ds(w * 128, 128)] = g

    for c in sent:
        c.wait_send()

    @pl.loop(0, NY - 1)
    def _(k):
        scatter(k, None).wait_send()
        gather(k, None).wait_send()

    @pl.loop(1, N_REL)
    def _(k):
        p = lax.rem(rel + k, N_REL)
        rcopy(send_buf.at[p], recv.at[rel], a_s.at[k], a_r.at[rel], {"rel": p}).wait_send()
        rcopy(gt.at[p], ret.at[rel], b_s.at[k], b_r.at[rel], {"rel": p}).wait_send()

    @pl.loop(0, ZX - 1)
    def _(k):
        p = zx_peer(k)
        here = nbuf.at[mine, zi]
        rcopy(here, here, s2_s.at[k], s2_r.at[zi], zx_dev(p)).wait_send()
        rcopy(ring.at[y, p], zx_recv.at[zi], z_s.at[k], z_r.at[zi], zx_dev(p)).wait_send()

    @pl.loop(1, NY)
    def _(k):
        to = {"dom": zh * NY + lax.rem(y + k, NY)}
        rcopy(rel_full.at[y], rel_full.at[y], ra_s.at[k], ra_r.at[y], to).wait_send()


def shards(
    entity, entity_acc, relation, relation_acc, send_rows, trip_head, trip_rel, trip_tail, neg_part, neg_rows,
):
    send_t = send_rows[0].T
    row = (1, TRIP)
    anywhere = pl.BlockSpec(memory_space=pl.ANY)
    vmem = pl.BlockSpec(memory_space=pltpu.VMEM)
    dma = pltpu.SemaphoreType.DMA
    rows = jax.ShapeDtypeStruct((ENT, WIDTH), F32)
    grad_e, grad_r = pl.pallas_call(
        kernel,
        out_shape=(rows, rows),
        in_specs=[anywhere] * 8,
        out_specs=(vmem, vmem),
        scratch_shapes=[
            pltpu.VMEM((ENT, WIDTH), F32),
            pltpu.VMEM((RELS, WIDTH), F32),
            pltpu.VMEM((SLOTS, N_REL), jnp.int32),
            pltpu.VMEM(row, jnp.int32),
            pltpu.VMEM(row, jnp.int32),
            pltpu.VMEM(row, jnp.int32),
            pltpu.VMEM((N_REL, NEG), jnp.int32),
            pltpu.VMEM((1, 1), jnp.int32),
            pltpu.VMEM((N_REL, SLOTS, WIDTH), F32),
            pltpu.VMEM((N_REL, SLOTS, WIDTH), F32),
            pltpu.VMEM((NY, 2, *TILE), F32),
            pltpu.VMEM((NY, 2, *TILE), F32),
            pltpu.VMEM((2 * NY, ZX, *TILE), F32),
            pltpu.VMEM((N_REL * SLOTS, 2 * TRIP), BF16),
            pltpu.VMEM((2 * TRIP, WIDTH), F32),
            pltpu.VMEM((TRIP, WIDTH), F32),
            pltpu.VMEM((TRIP, WIDTH), F32),
            pltpu.VMEM((TRIP, WIDTH), F32),
            pltpu.VMEM((2 * TRIP, WIDTH), F32),
            pltpu.VMEM((RELS, TRIP), BF16),
            pltpu.VMEM((RELS, WIDTH), F32),
            pltpu.VMEM((RELS, WIDTH // 4), F32),
            pltpu.VMEM((TRIP, WIDTH), BF16),
            pltpu.VMEM((TRIP, WIDTH), BF16),
            pltpu.VMEM((NY, 8, *TILE), F32),
            pltpu.VMEM((4, 8, *TILE), F32),
            pltpu.VMEM((4, 8, *TILE), F32),
            pltpu.VMEM((2 * NY, ZX, *TILE), F32),
            pltpu.VMEM((NY, ZX, *TILE), F32),
            pltpu.VMEM((NY, ZX, *TILE), F32),
            pltpu.VMEM((4, ZX, *TILE), F32),
            pltpu.VMEM((4, ZX, *TILE), F32),
            pltpu.VMEM((ZX, *TILE), F32),
            pltpu.VMEM((8, *TILE), F32),
            pltpu.VMEM((2, *TILE), F32),
            pltpu.VMEM(TILE, F32),
            pltpu.VMEM((NY, 2, *TILE), F32),
            pltpu.VMEM((NY, 8, *TILE), F32),
            pltpu.VMEM((N_REL, SLOTS, WIDTH), F32),
            pltpu.VMEM((N_REL, SLOTS, WIDTH), F32),
            dma((8,)), dma((N_REL,)), dma((N_REL,)), dma((N_REL,)), dma((N_REL,)),
            dma((NY,)), dma((NY,)), dma((ZX,)), dma((ZX,)),
            dma((8,)), dma((8,)), dma((8,)), dma((8,)),
            dma((16,)), dma((16,)), dma((2,)), dma((2,)),
            dma((8,)), dma((8,)), dma((8,)), dma((8,)),
            dma((ZX,)), dma((ZX,)), dma, dma,
            dma((NY,)), dma((NY,)), dma((NY,)), dma((NY,)),
            dma((4,)), dma((4,)), dma((4,)), dma((4,)), dma((2,)), dma((2,)),
        ],
        compiler_params=pltpu.CompilerParams(
            collective_id=0, has_side_effects=True, vmem_limit_bytes=56 << 20
        ),
        name="step",
    )(
        entity, relation, send_t, trip_head.reshape(row), trip_tail.reshape(row),
        trip_rel.reshape(row), neg_rows, neg_part.reshape(1, 1),
    )
    return (
        *adagrad(entity, entity_acc, grad_e),
        *adagrad(relation, relation_acc, grad_r),
    )


def solution(mesh):
    both = ("dom", "rel")
    in_specs = (
        P(both, None), P(both, None), P("rel", None), P("rel", None), P(both, None, None),
        P(both), P(both), P(both), P(), P(),
    )
    out_specs = (P(both, None), P(both, None), P("rel", None), P("rel", None))
    return jax.shard_map(shards, mesh=mesh, in_specs=in_specs, out_specs=out_specs, check_vma=False)
```

```python
import jax
import jax.numpy as jnp
from jax import lax
from jax.experimental import pallas as pl
from jax.experimental.pallas import tpu as pltpu
from jax.sharding import PartitionSpec as P

MESH = pl.DeviceIdType.MESH
F32, BF16 = jnp.float32, jnp.bfloat16
step_size = 0.05

N_DOM, N_REL = 16, 32
NY, NX = 8, 4
ZX = 32
ENT, RELS, TRIP, SLOTS, NEG, WIDTH = 128, 128, 256, 16, 32, 512
TILE = (8, 128)
NEGS = NEG * N_REL
AHEAD = (8, 12, 15, 18, 21, 24, 27, 32)
BACK = (12, 15, 18, 20, 22, 24, 32)
HALF = ZX // 2

NN = (((1,), (0,)), ((), ()))
TN = (((0,), (0,)), ((), ()))
NT = (((1,), (1,)), ((), ()))


def mm(a, b, dims):
    return lax.dot_general(a, b, dims, preferred_element_type=F32)


def halves(v):
    hi = v.astype(BF16)
    return hi, (v - hi.astype(F32)).astype(BF16)


def select(one_hot, v, dims):
    hi, lo = halves(v)
    return mm(one_hot, hi, dims) + mm(one_hot, lo, dims)


def mm3(a, b, dims):
    return mm(a[0], b[0], dims) + (mm(a[0], b[1], dims) + mm(a[1], b[0], dims))


def hot(rows, index_row):
    n = index_row.shape[1]
    at = lax.broadcasted_iota(jnp.int32, (rows, n), 0)
    return jnp.where(at == index_row, 1.0, 0.0).astype(BF16)


def slot_row(send_t):
    n = N_REL * SLOTS
    at = lax.broadcasted_iota(jnp.int32, (N_REL, n), 1)
    spread = lax.div(at, SLOTS) == lax.broadcasted_iota(jnp.int32, (N_REL, n), 0)
    full = mm(
        send_t[...].astype(F32).astype(BF16), jnp.where(spread, 1.0, 0.0).astype(BF16), NN
    )
    slot = lax.rem(lax.broadcasted_iota(jnp.int32, (SLOTS, n), 1), SLOTS)
    keep = slot == lax.broadcasted_iota(jnp.int32, (SLOTS, n), 0)
    return jnp.sum(jnp.where(keep, full, 0.0), axis=0, keepdims=True).astype(jnp.int32)


def rcopy(src, dst, ssem, rsem, dev):
    return pltpu.make_async_remote_copy(
        src_ref=src, dst_ref=dst, send_sem=ssem, recv_sem=rsem, device_id=dev, device_id_type=MESH
    )


def quarter(v):
    return v[:, 0:128], v[:, 128:256], v[:, 256:384], v[:, 384:512]


def adagrad(values, history, gradient):
    history_new = history + gradient * gradient
    return values - step_size * gradient / jnp.sqrt(history_new), history_new


def kernel(
    entity_h, relation_h, send_h, head_h, tail_h, rels_h, neg_h, part_h,
    grad_e, grad_r,
    entity, relation, send_t, head_row, tail_row, rels_row, neg_rows, neg_part,
    send_buf, recv, neg_src, s1_recv, nbuf, hot_ends, ends, rot, query, dq, dends,
    rel_hot, unit, scale, q_hi, q_lo, rring, rrp, rrm,
    gall, xrecv, ring, rp, rm, zx_recv, relx, tile_out, t_recv, rel_full, gt, ret,
    in_s, a_s, a_r, b_s, b_r, s1_s, s1_r, s2_s, s2_r, yp_s, yp_r, ym_s, ym_r, sib_s, sib_r, x_s, x_r,
    rp_s, rp_r, rm_s, rm_r, z_s, z_r, rx_s, rx_r, t_s, t_r, ra_s, ra_r,
    up_s, up_r, dn_s, dn_r,
):
    loads = [
        pltpu.make_async_copy(h, v, in_s.at[n])
        for n, (h, v) in enumerate(
            (
                (entity_h, entity), (neg_h, neg_rows), (send_h, send_t), (part_h, neg_part),
                (head_h, head_row), (tail_h, tail_row), (rels_h, rels_row), (relation_h, relation),
            )
        )
    ]
    for c in loads:
        c.start()
    dom, rel = lax.axis_index("dom"), lax.axis_index("rel")
    zh, y = lax.div(dom, NY), lax.rem(dom, NY)
    zx_low, core = lax.div(rel, 2), lax.rem(rel, 2)
    zi = zh * 16 + zx_low
    up, down = lax.rem(y + 1, NY), lax.rem(y + NY - 1, NY)
    up_dev, down_dev = {"dom": zh * NY + up}, {"dom": zh * NY + down}
    sib_dev = {"rel": zx_low * 2 + (1 - core)}

    def zx_dev(p):
        return {"dom": lax.div(p, 16) * NY + y, "rel": lax.rem(p, 16) * 2 + core}

    def fan(j, n):
        return n // 2 + lax.div(j + 1, 2) * (1 - 2 * lax.rem(j, 2))

    def zx_peer(j):
        return lax.rem(zi + fan(j, ZX), ZX)

    def dom_peer(j):
        other = lax.rem(zh + 1 - lax.div(j, NY), 2)
        return other * NY + lax.rem(y + fan(lax.rem(j, NY), NY), NY)

    barrier = pltpu.get_barrier_semaphore()

    @pl.loop(0, N_DOM - 1)
    def _(k):
        pl.semaphore_signal(
            barrier, inc=1, device_id={"dom": dom_peer(k)}, device_id_type=MESH
        )

    @pl.loop(1, N_REL)
    def _(k):
        pl.semaphore_signal(
            barrier, inc=1, device_id={"rel": lax.rem(rel + k, N_REL)}, device_id_type=MESH
        )

    @pl.loop(1, 16)
    def _(k):
        p = (1 - zh) * 16 + lax.rem(zx_low + k, 16)
        pl.semaphore_signal(barrier, inc=1, device_id=zx_dev(p), device_id_type=MESH)

    for c in loads[:4]:
        c.wait()
    ent = halves(entity[...])
    neg_hot = hot(ENT, neg_rows[pl.ds(rel, 1), :])
    own = mm(neg_hot, ent[0], TN) + mm(neg_hot, ent[1], TN)
    for g in range(4):
        for w in range(4):
            neg_src[g * 4 + w] = own[g * 8 : g * 8 + 8, w * 128 : w * 128 + 128]
    send_hot = hot(ENT, slot_row(send_t))
    rows = mm(send_hot, ent[0], TN) + mm(send_hot, ent[1], TN)
    send_buf[...] = rows.reshape(N_REL, SLOTS, WIDTH)
    for c in loads[4:]:
        c.wait()
    is_root = lax.broadcasted_iota(jnp.int32, (N_DOM, 1, 1), 0) == neg_part[...].reshape(1, 1, 1)

    pl.semaphore_wait(barrier, (N_DOM - 1) + (N_REL - 1) + 15)

    @pl.loop(0, N_DOM - 1)
    def _(k):
        p = dom_peer(k)
        rcopy(neg_src.at[p], s1_recv.at[dom], s1_s.at[k], s1_r.at[dom], {"dom": p}).start()

    def peer(k):
        pz = lax.rem(lax.div(rel, 8) + lax.rem(k, 4), 4)
        px = lax.rem(lax.div(lax.rem(rel, 8), 2) + lax.div(k, 8), NX)
        pc = lax.rem(core + lax.rem(lax.div(k, 4), 2), 2)
        return pz * 8 + px * 2 + pc

    def exchange(src, dst, ssem, rsem, lo, hi):
        @pl.loop(lo, hi)
        def _(k):
            p = peer(k)
            rcopy(src.at[p], dst.at[rel], ssem.at[k], rsem.at[rel], {"rel": p}).start()

    def ahead(n):
        exchange(send_buf, recv, a_s, a_r, AHEAD[n - 1] if n else 1, AHEAD[n])

    def back(n):
        exchange(gt, ret, b_s, b_r, BACK[n - 1] if n else 1, BACK[n])

    ahead(0)

    s1_recv[dom] = neg_src[dom]
    recv[rel] = send_buf[rel]

    @pl.loop(0, N_DOM - 1)
    def _(k):
        p = dom_peer(k)
        rcopy(neg_src.at[p], s1_recv.at[p], s1_s.at[k], s1_r.at[p], {"dom": p}).wait_recv()

    mine = core * NY + y
    nbuf[mine, zi] = jnp.sum(jnp.where(is_root, s1_recv[...], 0.0), axis=0)

    @pl.loop(0, ZX - 1)
    def _(k):
        p = zx_peer(k)
        here = nbuf.at[mine, zi]
        rcopy(here, here, s2_s.at[k], s2_r.at[zi], zx_dev(p)).start()

    ahead(1)

    @pl.loop(0, ZX - 1)
    def _(k):
        p = zx_peer(k)
        there = nbuf.at[mine, p]
        rcopy(there, there, s2_s.at[k], s2_r.at[p], zx_dev(p)).wait_recv()

    def part(core_of, yy, h):
        return nbuf.at[core_of * NY + lax.rem(yy + 2 * NY, NY), pl.ds(h * HALF, HALF)]

    def pass_up(yy, h, n):
        ref = part(core, yy, h)
        return rcopy(ref, ref, yp_s.at[2 * n + h], yp_r.at[2 * n + h], up_dev)

    def pass_down(yy, h, n):
        ref = part(core, yy, h)
        return rcopy(ref, ref, ym_s.at[2 * n + h], ym_r.at[2 * n + h], down_dev)

    def to_sib(core_of, off, h):
        ref = part(core_of, y + off, h)
        at = 2 * (off + 4) + h
        return rcopy(ref, ref, sib_s.at[at], sib_r.at[at], sib_dev)

    sent = []

    def go(c):
        c.start()
        sent.append(c)

    for h in (0, 1):
        go(pass_up(y, h, 0))
        go(pass_down(y, h, 0))
    for h in (0, 1):
        go(to_sib(core, 0, h))
    for n in (1, 2, 3):
        for h in (0, 1):
            pass_up(y - n, h, n - 1).wait_recv()
            if n < 3 or h == 0:
                go(pass_up(y - n, h, n))
            go(to_sib(core, -n, h))
            pass_down(y + n, h, n - 1).wait_recv()
            if n < 3 or h == 1:
                go(pass_down(y + n, h, n))
            go(to_sib(core, n, h))
            ahead(2 * n + h)

    rel_hot[...] = hot(RELS, rels_row[...])
    ra, rb, rc, rd = quarter(relation[...])
    inv = 1.0 / jnp.sqrt(ra * ra + rb * rb + rc * rc + rd * rd)
    scale[...] = inv
    unit[...] = jnp.concatenate([ra * inv, rb * inv, rc * inv, rd * inv], axis=1)
    rot[...] = select(rel_hot[...], unit[...], TN)
    hot_ends[:, pl.ds(0, TRIP)] = hot(N_REL * SLOTS, head_row[...])
    hot_ends[:, pl.ds(TRIP, TRIP)] = hot(N_REL * SLOTS, tail_row[...])

    @pl.loop(1, N_REL)
    def _(k):
        p = lax.rem(rel + k, N_REL)
        rcopy(send_buf.at[p], recv.at[p], a_s.at[k], a_r.at[p], {"rel": p}).wait_recv()

    ends[...] = select(hot_ends[...], recv[...].reshape(N_REL * SLOTS, WIDTH), TN)
    ha, hb, hc, hd = quarter(ends[pl.ds(0, TRIP), :])
    ua, ub, uc, ud = quarter(rot[...])
    qa = ha * ua - hb * ub - hc * uc - hd * ud
    qb = ha * ub + hb * ua + hc * ud - hd * uc
    qc = ha * uc - hb * ud + hc * ua + hd * ub
    qd = ha * ud + hb * uc - hc * ub + hd * ua
    query[...] = jnp.concatenate([qa, qb, qc, qd], axis=1)
    q_hi[...], q_lo[...] = halves(query[...])
    tails = ends[pl.ds(TRIP, TRIP), :]
    positive = jnp.sum(query[...] * tails, axis=1, keepdims=True)
    pull = -1.0 / (1.0 + jnp.exp(positive))
    dq[...] = pull * tails
    dends[pl.ds(TRIP, TRIP), :] = pull * query[...]

    pass_up(y - 4, 0, 3).wait_recv()
    go(to_sib(core, -4, 0))
    pass_down(y + 4, 1, 3).wait_recv()
    go(to_sib(core, -4, 1))
    def score(b):
        q = q_hi[...], q_lo[...]
        n = halves(
            jnp.concatenate(
                [nbuf[b * 4 + w].reshape(ZX * 8, 128) for w in range(4)], axis=1
            )
        )
        s = mm3(q, n, NT)
        p = halves((1.0 / NEGS) / (1.0 + jnp.exp(-s)))
        dq[...] += mm3(p, n, NN)
        dn = mm3(p, q, TN)
        for w in range(4):
            gall[b * 4 + w] = dn[:, w * 128 : w * 128 + 128].reshape(ZX, 8, 128)

    def swap(of, h):
        src = gall.at[pl.ds(of * NY + 4 * h, 4)]
        return rcopy(src, xrecv.at[pl.ds(4 * h, 4)], x_s.at[h], x_r.at[h], sib_dev)

    def chunk(yy, h):
        return ring.at[lax.rem(yy + 2 * NY, NY), pl.ds(h * HALF, HALF)]

    def take(yy, h, got, n):
        i = lax.rem(yy + 2 * NY, NY)
        cols = pl.ds(h * HALF, HALF)
        ring[i, cols] = ring[i, cols] + got[n, cols]

    def sum_up(yy, h, n):
        at = 2 * n + h
        dst = rp.at[n, pl.ds(h * HALF, HALF)]
        return rcopy(chunk(yy, h), dst, rp_s.at[at], rp_r.at[at], up_dev)

    def sum_down(yy, h, n):
        at = 2 * n + h
        dst = rm.at[n, pl.ds(h * HALF, HALF)]
        return rcopy(chunk(yy, h), dst, rm_s.at[at], rm_r.at[at], down_dev)

    def neg_step(n, h):
        sum_up(y + 4 - n, h, n - 1).wait_recv()
        take(y + 4 - n, h, rp, n - 1)
        go(sum_up(y + 4 - n, h, n))
        sum_down(y - 4 + n, 1 - h, n - 1).wait_recv()
        take(y - 4 + n, 1 - h, rm, n - 1)
        go(sum_down(y - 4 + n, 1 - h, n))

    def rel_up(n):
        cols = pl.ds(0, 8 if n else 4)
        src = rring.at[lax.rem(y + 4 - n, NY), cols]
        return rcopy(src, rrp.at[n, cols], up_s.at[n], up_r.at[n], up_dev)

    def rel_down(n):
        cols = pl.ds(0, 8) if n else pl.ds(4, 4)
        src = rring.at[lax.rem(y + 4 + n, NY), cols]
        return rcopy(src, rrm.at[n, cols], dn_s.at[n], dn_r.at[n], down_dev)

    def rel_step(n):
        u, d = lax.rem(y + 4 - n, NY), lax.rem(y + 4 + n, NY)
        uc, dc = (pl.ds(0, 4), pl.ds(4, 4)) if n == 1 else (pl.ds(0, 8), pl.ds(0, 8))
        rel_up(n - 1).wait_recv()
        rring[u, uc] = rring[u, uc] + rrp[n - 1, uc]
        go(rel_up(n))
        rel_down(n - 1).wait_recv()
        rring[d, dc] = rring[d, dc] + rrm[n - 1, dc]
        go(rel_down(n))

    def merge(h):
        swap(core, h).wait_recv()

        @pl.loop(0, 4)
        def _(k):
            i = h * 4 + k
            ring[i] = gall[core * NY + i] + xrecv[i]

    near = lax.div(y, 4)
    away = 1 - near
    score(core * 2 + away)
    for off in (0, -1, 1, -2, 2, -3, 3, -4):
        for h in (0, 1):
            to_sib(1 - core, off, h).wait_recv()
    score((1 - core) * 2 + away)
    go(swap(1 - core, away))
    score((1 - core) * 2 + near)
    go(swap(1 - core, near))
    merge(away)
    go(sum_up(y + 4, 0, 0))
    go(sum_down(y - 4, 1, 0))
    score(core * 2 + near)
    merge(near)
    go(sum_up(y + 3, 1, 1))
    go(sum_down(y - 3, 0, 1))

    ga, gb, gc, gd = quarter(dq[...])
    ha, hb, hc, hd = quarter(ends[pl.ds(0, TRIP), :])
    ua, ub, uc, ud = quarter(rot[...])
    dha = ga * ua + gb * ub + gc * uc + gd * ud
    dhb = gb * ua - ga * ub - gc * ud + gd * uc
    dhc = gb * ud - ga * uc + gc * ua - gd * ub
    dhd = gc * ub - ga * ud - gb * uc + gd * ua
    dends[pl.ds(0, TRIP), :] = jnp.concatenate([dha, dhb, dhc, dhd], axis=1)
    gt[...] = select(hot_ends[...], dends[...], NN).reshape(N_REL, SLOTS, WIDTH)

    ret[rel] = gt[rel]
    back(0)
    neg_step(1, 0)
    back(1)
    dua = ga * ha + gb * hb + gc * hc + gd * hd
    dub = gb * ha - ga * hb + gc * hd - gd * hc
    duc = gc * ha - ga * hc - gb * hd + gd * hb
    dud = gb * hc - ga * hd - gc * hb + gd * ha
    du = select(rel_hot[...], jnp.concatenate([dua, dub, duc, dud], axis=1), NN)
    va, vb, vc, vd = quarter(unit[...])
    inv = scale[...]
    da, db, dc, dd = quarter(du)
    along = da * va + db * vb + dc * vc + dd * vd
    parts = [(g - v * along) * inv for g, v in ((da, va), (db, vb), (dc, vc), (dd, vd))]
    for yy in range(NY):
        for g in range(2):
            for w in range(4):
                at = yy * 16 + g * 8
                rring[yy, g * 4 + w] = parts[w][at : at + 8, :]
    go(rel_up(0))
    go(rel_down(0))

    for n in (2, 3):
        for h in (1, 0):
            neg_step(n, h)
            back(2 * n - 1 - h)
        rel_step(n - 1)
    for h in (1, 0):
        sum_up(y, h, 3).wait_recv()
        sum_down(y, 1 - h, 3).wait_recv()
    ring[y] = ring[y] + (rp[3] + rm[3])

    far = {"dom": (1 - zh) * NY + y}
    cross = rcopy(rring.at[y], relx, rx_s, rx_r, far)

    @pl.loop(0, ZX - 1)
    def _(k):
        p = zx_peer(k)
        rcopy(ring.at[y, p], zx_recv.at[zi], z_s.at[k], z_r.at[zi], zx_dev(p)).start()

    rel_step(3)
    rel_up(3).wait_recv()
    rel_down(3).wait_recv()
    rring[y] = rring[y] + (rrp[3] + rrm[3])
    go(cross)
    back(6)
    zx_recv[zi] = ring[y, zi]

    @pl.loop(0, ZX - 1)
    def _(k):
        p = zx_peer(k)
        rcopy(ring.at[y, p], zx_recv.at[p], z_s.at[k], z_r.at[p], zx_dev(p)).wait_recv()

    tile_out[...] = jnp.sum(zx_recv[...], axis=0)

    @pl.loop(0, N_DOM - 1)
    def _(k):
        p = dom_peer(k)
        rcopy(tile_out, t_recv.at[dom], t_s.at[k], t_r.at[dom], {"dom": p}).start()

    t_recv[dom] = tile_out[...]
    cross.wait_recv()
    rel_full[y] = rring[y] + relx[...]

    @pl.loop(1, NY)
    def _(k):
        to = {"dom": zh * NY + lax.rem(y + k, NY)}
        rcopy(rel_full.at[y], rel_full.at[y], ra_s.at[k], ra_r.at[y], to).start()

    @pl.loop(1, N_REL)
    def _(k):
        p = lax.rem(rel + k, N_REL)
        rcopy(gt.at[p], ret.at[p], b_s.at[k], b_r.at[p], {"rel": p}).wait_recv()

    send_hot = hot(ENT, slot_row(send_t))
    grad = select(send_hot, ret[...].reshape(N_REL * SLOTS, WIDTH), NN)

    @pl.loop(0, N_DOM - 1)
    def _(k):
        p = dom_peer(k)
        rcopy(tile_out, t_recv.at[p], t_s.at[k], t_r.at[p], {"dom": p}).wait_recv()

    total = jnp.concatenate(
        [
            jnp.concatenate([t_recv[g * 4 + w] for w in range(4)], axis=1)
            for g in range(4)
        ],
        axis=0,
    )
    owner = jnp.where(neg_part[...] == dom, 1.0, 0.0).astype(F32)
    neg_hot = hot(ENT, neg_rows[pl.ds(rel, 1), :])
    grad_e[...] = grad + owner * select(neg_hot, total, NN)

    @pl.loop(1, NY)
    def _(k):
        i = lax.rem(y + k, NY)
        there = rel_full.at[i]
        rcopy(there, there, ra_s.at[k], ra_r.at[i], {"dom": zh * NY + i}).wait_recv()

    for w in range(4):
        g = jnp.concatenate(
            [rel_full[yy, gg * 4 + w] for yy in range(NY) for gg in range(2)], axis=0
        )
        grad_r[:, pl.ds(w * 128, 128)] = g

    for c in sent:
        c.wait_send()

    @pl.loop(0, N_DOM - 1)
    def _(k):
        p = dom_peer(k)
        rcopy(neg_src.at[p], s1_recv.at[dom], s1_s.at[k], s1_r.at[dom], {"dom": p}).wait_send()
        rcopy(tile_out, t_recv.at[dom], t_s.at[k], t_r.at[dom], {"dom": p}).wait_send()

    @pl.loop(1, N_REL)
    def _(k):
        p = lax.rem(rel + k, N_REL)
        rcopy(send_buf.at[p], recv.at[rel], a_s.at[k], a_r.at[rel], {"rel": p}).wait_send()
        rcopy(gt.at[p], ret.at[rel], b_s.at[k], b_r.at[rel], {"rel": p}).wait_send()

    @pl.loop(0, ZX - 1)
    def _(k):
        p = zx_peer(k)
        here = nbuf.at[mine, zi]
        rcopy(here, here, s2_s.at[k], s2_r.at[zi], zx_dev(p)).wait_send()
        rcopy(ring.at[y, p], zx_recv.at[zi], z_s.at[k], z_r.at[zi], zx_dev(p)).wait_send()

    @pl.loop(1, NY)
    def _(k):
        to = {"dom": zh * NY + lax.rem(y + k, NY)}
        rcopy(rel_full.at[y], rel_full.at[y], ra_s.at[k], ra_r.at[y], to).wait_send()


def shards(
    entity, entity_acc, relation, relation_acc, send_rows, trip_head, trip_rel, trip_tail, neg_part, neg_rows,
):
    send_t = send_rows[0].T
    row = (1, TRIP)
    anywhere = pl.BlockSpec(memory_space=pl.ANY)
    vmem = pl.BlockSpec(memory_space=pltpu.VMEM)
    dma = pltpu.SemaphoreType.DMA
    rows = jax.ShapeDtypeStruct((ENT, WIDTH), F32)
    grad_e, grad_r = pl.pallas_call(
        kernel,
        out_shape=(rows, rows),
        in_specs=[anywhere] * 8,
        out_specs=(vmem, vmem),
        scratch_shapes=[
            pltpu.VMEM((ENT, WIDTH), F32),
            pltpu.VMEM((RELS, WIDTH), F32),
            pltpu.VMEM((SLOTS, N_REL), jnp.int32),
            pltpu.VMEM(row, jnp.int32),
            pltpu.VMEM(row, jnp.int32),
            pltpu.VMEM(row, jnp.int32),
            pltpu.VMEM((N_REL, NEG), jnp.int32),
            pltpu.VMEM((1, 1), jnp.int32),
            pltpu.VMEM((N_REL, SLOTS, WIDTH), F32),
            pltpu.VMEM((N_REL, SLOTS, WIDTH), F32),
            pltpu.VMEM((N_DOM, *TILE), F32),
            pltpu.VMEM((N_DOM, *TILE), F32),
            pltpu.VMEM((2 * NY, ZX, *TILE), F32),
            pltpu.VMEM((N_REL * SLOTS, 2 * TRIP), BF16),
            pltpu.VMEM((2 * TRIP, WIDTH), F32),
            pltpu.VMEM((TRIP, WIDTH), F32),
            pltpu.VMEM((TRIP, WIDTH), F32),
            pltpu.VMEM((TRIP, WIDTH), F32),
            pltpu.VMEM((2 * TRIP, WIDTH), F32),
            pltpu.VMEM((RELS, TRIP), BF16),
            pltpu.VMEM((RELS, WIDTH), F32),
            pltpu.VMEM((RELS, WIDTH // 4), F32),
            pltpu.VMEM((TRIP, WIDTH), BF16),
            pltpu.VMEM((TRIP, WIDTH), BF16),
            pltpu.VMEM((NY, 8, *TILE), F32),
            pltpu.VMEM((4, 8, *TILE), F32),
            pltpu.VMEM((4, 8, *TILE), F32),
            pltpu.VMEM((2 * NY, ZX, *TILE), F32),
            pltpu.VMEM((NY, ZX, *TILE), F32),
            pltpu.VMEM((NY, ZX, *TILE), F32),
            pltpu.VMEM((4, ZX, *TILE), F32),
            pltpu.VMEM((4, ZX, *TILE), F32),
            pltpu.VMEM((ZX, *TILE), F32),
            pltpu.VMEM((8, *TILE), F32),
            pltpu.VMEM(TILE, F32),
            pltpu.VMEM((N_DOM, *TILE), F32),
            pltpu.VMEM((NY, 8, *TILE), F32),
            pltpu.VMEM((N_REL, SLOTS, WIDTH), F32),
            pltpu.VMEM((N_REL, SLOTS, WIDTH), F32),
            dma((8,)), dma((N_REL,)), dma((N_REL,)), dma((N_REL,)), dma((N_REL,)),
            dma((N_DOM,)), dma((N_DOM,)), dma((ZX,)), dma((ZX,)),
            dma((8,)), dma((8,)), dma((8,)), dma((8,)),
            dma((16,)), dma((16,)), dma((2,)), dma((2,)),
            dma((8,)), dma((8,)), dma((8,)), dma((8,)),
            dma((ZX,)), dma((ZX,)), dma, dma,
            dma((N_DOM,)), dma((N_DOM,)), dma((NY,)), dma((NY,)),
            dma((4,)), dma((4,)), dma((4,)), dma((4,)),
        ],
        compiler_params=pltpu.CompilerParams(
            collective_id=0, has_side_effects=True, vmem_limit_bytes=56 << 20
        ),
        name="step",
    )(
        entity, relation, send_t, trip_head.reshape(row), trip_tail.reshape(row),
        trip_rel.reshape(row), neg_rows, neg_part.reshape(1, 1),
    )
    return (
        *adagrad(entity, entity_acc, grad_e),
        *adagrad(relation, relation_acc, grad_r),
    )


def solution(mesh):
    both = ("dom", "rel")
    in_specs = (
        P(both, None), P(both, None), P("rel", None), P("rel", None), P(both, None, None),
        P(both), P(both), P(both), P(), P(),
    )
    out_specs = (P(both, None), P(both, None), P("rel", None), P("rel", None))
    return jax.shard_map(shards, mesh=mesh, in_specs=in_specs, out_specs=out_specs, check_vma=False)
```
